512 devices in a mesh: cluster: 64 (over y, z), copy: 8 (over x, core).
Axes of the slice: x: 4, y: 8, z: 8, core: 2. Of those that a mesh axis runs over, the one named last changes fastest.
Arguments:
- points: bfloat16 [8192, 128, 512], P(('cluster', 'copy')), may hold values from -18 to 18
- block_ids: int32 [8192], P(('cluster', 'copy')), may hold values from 0 to 63, as said below
- block_counts: int32 [512], P(('cluster', 'copy')), may hold values from 11 to 16, as said below
- centroids: bfloat16 [131072, 512], P('cluster'), may hold values from -6 to 6
Outputs:
- new_centroids: bfloat16 [131072, 512], P(('cluster', 'copy'))
The draws below stay inside these ranges and needn't reach their ends.
Inputs may be any that keep to these rules, and one draw needn't show every extreme that they name: `block_ids`: the 16 blocks of one device name 16 different coarse clusters. For every index along copy, one coarse cluster is named by the first block of every device with that copy index. Only the first block_counts[d] block slots of device d are valid. Some device has all 16 valid.
All inputs are finite; a program needn't handle non-finite values.
Results may differ from the reference program's by a relative error of at most 0.0021.
Values may be sent and summed in bfloat16 or wider, within the bound.
A program may use at most 64 MiB of HBM per device.

```python
import math
import jax
import jax.numpy as jnp
from jax import lax

D = 512
K = 2048
BLOCK = 128
NB = 16
N_CLUSTER = 64
N_COPY = 8
DEVICES = 512


def route_table(key):
    favorite = jax.random.randint(jax.random.fold_in(key, 101), (N_COPY,), 0, N_CLUSTER)
    levels = jax.random.randint(jax.random.fold_in(key, 102), (N_CLUSTER,), 1, 5)
    lottery = jax.random.randint(jax.random.fold_in(key, 103), (DEVICES, N_CLUSTER), 0, 65536)
    owner_ids = jnp.arange(N_CLUSTER, dtype=jnp.int32)
    scores = lottery * levels[None, :] * N_CLUSTER + owner_ids[None, :]
    replica = jnp.arange(DEVICES, dtype=jnp.int32) % N_COPY
    preferred = owner_ids[None, :] == favorite[replica][:, None]
    scores = jnp.where(preferred, jnp.int32(1 << 30), scores).astype(jnp.int32)
    chosen = lax.top_k(scores, NB)[1].astype(jnp.int32)
    return chosen


def draw_block_ids(key, part):
    return route_table(key).reshape(DEVICES * NB)


def draw_block_counts(key, part):
    lowest = NB - NB * 5 // 16
    counts_drawn = jax.random.randint(jax.random.fold_in(key, 104), (DEVICES,), lowest, NB + 1)
    fullest = jax.random.randint(jax.random.fold_in(key, 105), (), 0, DEVICES)
    return jnp.where(jnp.arange(DEVICES) == fullest, NB, counts_drawn).astype(jnp.int32)


def draw_centroids(key, part):
    normal_draw = jax.random.normal(jax.random.fold_in(key, 108), (N_CLUSTER * K, D), jnp.float32)
    return jnp.clip(normal_draw, -6.0, 6.0).astype(jnp.bfloat16)


def draw_points(key, part):
    extent = (DEVICES * NB, BLOCK, D)
    normal_draw = jax.random.normal(jax.random.fold_in(key, 113), extent, jnp.float32)
    return jnp.clip(normal_draw, -6.0, 6.0).astype(jnp.bfloat16)


def setup_inputs(seed: int = 0) -> dict:
    splits = jax.random.split(jax.random.key(seed), 5)
    points = draw_points(jax.random.fold_in(splits[4], 71), 0)
    block_ids = draw_block_ids(jax.random.fold_in(splits[4], 71), 0)
    block_counts = draw_block_counts(jax.random.fold_in(splits[4], 71), 0)
    centroids = draw_centroids(jax.random.fold_in(splits[4], 71), 0)
    return {"points": points, "block_ids": block_ids, "block_counts": block_counts, "centroids": centroids}


turn_blocks = 4

def cluster_sums(points, block_ids, block_counts, cluster_rows, cluster):
    devices_all = block_counts.shape[0]
    id_table = block_ids.reshape(devices_all, NB)
    slot_index = jnp.arange(NB, dtype=jnp.int32)
    in_range = slot_index[None, :] < block_counts[:, None]
    matches = (id_table == cluster) & in_range
    holder = jnp.any(matches, axis=1)
    position = lax.optimization_barrier(jnp.sum(jnp.where(matches, slot_index[None, :], 0), axis=1)).astype(jnp.int32)
    flat_index = (jnp.arange(devices_all, dtype=jnp.int32) * NB + position).astype(jnp.int32)
    ranking = (jnp.cumsum(holder.astype(jnp.int32)) - 1).astype(jnp.int32)
    listing = jnp.zeros((devices_all + turn_blocks,), jnp.int32)
    listing = listing.at[jnp.where(holder, ranking, devices_all + turn_blocks)].set(flat_index, mode='drop')
    how_many = jnp.sum(holder.astype(jnp.int32)).astype(jnp.int32)
    scale_factor = 3.0 / math.sqrt(D)

    def visit(step_index, running):
        start_at = (step_index * turn_blocks).astype(jnp.int32)
        chosen = lax.dynamic_slice_in_dim(listing, start_at, turn_blocks)
        usable = start_at + jnp.arange(turn_blocks, dtype=jnp.int32) < how_many
        gathered = points[chosen].reshape(turn_blocks * BLOCK, D)
        logits = jnp.dot(gathered, cluster_rows.T, preferred_element_type=jnp.float32) * scale_factor
        row_mask = jnp.repeat(usable, BLOCK).astype(jnp.float32)[:, None]
        weights = (jax.nn.softmax(logits, axis=-1) * row_mask).astype(jnp.bfloat16)
        return running + jnp.dot(weights.T, gathered, preferred_element_type=jnp.float32)
    initial = jnp.zeros((K, D), jnp.float32)
    upper = ((how_many + turn_blocks - 1) // turn_blocks).astype(jnp.int32)
    return lax.fori_loop(jnp.int32(0), upper, visit, initial)

def reference(points, block_ids, block_counts, centroids):
    grouped = centroids.reshape(N_CLUSTER, K, D)

    def per_cluster(cluster):
        cluster_rows = grouped[cluster]
        summed = cluster_sums(points, block_ids, block_counts, cluster_rows, cluster)
        combined = summed + cluster_rows.astype(jnp.float32)
        scaled = combined * lax.rsqrt(lax.optimization_barrier(jnp.mean(combined * combined, axis=-1, keepdims=True)) + 1e-06)
        return scaled.astype(jnp.bfloat16)
    updated = lax.map(per_cluster, jnp.arange(N_CLUSTER, dtype=jnp.int32))
    return updated.reshape(N_CLUSTER * K, D)
```

```python
import functools
import math

import jax
import jax.numpy as jnp
from jax import lax
from jax.experimental import pallas as pl
from jax.experimental.pallas import tpu as pltpu
from jax.sharding import PartitionSpec as P

MESH = pl.DeviceIdType.MESH
GROUP = 4
STRIDE = 27
TILE = 256


def kernel(
    shape, pos_ref, flag_ref, pts_ref, cent_ref, out_ref,
    stage, recv, logit, acc, pair, sbuf, rbuf,
    send_sem, recv_sem, pair_send, pair_recv, ring_send, ring_recv,
):
    slots, side, copies = shape
    rows, feature = cent_ref.shape
    share = rows // copies
    chips = copies // 2
    me = lax.axis_index("cluster")
    lane = lax.axis_index("copy")
    row, col = me // side, me % side
    chip, core = lane // 2, lane % 2
    partner = chip * 2 + (1 - core)

    def target(q):
        offset = (q * STRIDE) % slots
        return ((row + offset // side) % side) * side + (col + offset % side) % side

    barrier = pltpu.get_barrier_semaphore()

    def greet(q, carry):
        pl.semaphore_signal(barrier, inc=1, device_id=(target(q), lane), device_id_type=MESH)
        return carry

    lax.fori_loop(1, slots, greet, 0)
    pl.semaphore_signal(barrier, inc=1, device_id=(me, partner), device_id_type=MESH)
    for d in range(1, chips):
        other = ((chip + d) % chips) * 2 + core
        pl.semaphore_signal(barrier, inc=1, device_id=(me, other), device_id_type=MESH)

    recv[0] = pts_ref[pos_ref[me]] * flag_ref[me].astype(jnp.bfloat16)

    def fill(q, carry):
        k = target(q)
        stage[q] = pts_ref[pos_ref[k]] * flag_ref[k].astype(jnp.bfloat16)
        return carry

    lax.fori_loop(1, slots, fill, 0)
    acc[...] = jnp.zeros_like(acc)
    pl.semaphore_wait(barrier, slots - 1 + chips)

    def exchange(q):
        return pltpu.make_async_remote_copy(
            src_ref=stage.at[q],
            dst_ref=recv.at[q],
            send_sem=send_sem.at[q],
            recv_sem=recv_sem.at[q],
            device_id=(target(q), lane),
            device_id_type=MESH,
        )

    def begin(q, carry):
        exchange(q).start()
        return carry

    lax.fori_loop(1, slots, begin, 0)

    alpha = 3.0 / math.sqrt(feature) * math.log2(math.e)
    points = GROUP * pts_ref.shape[1]

    def step(j, carry):
        def arrive(b, carry):
            exchange(j * GROUP + b).wait_recv()
            return carry

        lax.fori_loop(jnp.where(j == 0, 1, 0), GROUP, arrive, 0)

        def block():
            return recv[pl.ds(j * GROUP, GROUP)].reshape(points, feature)

        def scores(r, top):
            at = pl.ds(pl.multiple_of(r * TILE, TILE), TILE)
            part = lax.dot_general(
                cent_ref[at, :], block(), (((1,), (1,)), ((), ())),
                preferred_element_type=jnp.float32,
            )
            logit[at, :] = part
            return jnp.maximum(top, jnp.max(part, axis=0, keepdims=True))

        top = lax.fori_loop(
            0, rows // TILE, scores, jnp.full((1, points), -jnp.inf, jnp.float32)
        ) * alpha

        def powers(r, total):
            at = pl.ds(pl.multiple_of(r * TILE, TILE), TILE)
            value = jnp.exp2(logit[at, :] * alpha - top)
            logit[at, :] = value
            return total + jnp.sum(value, axis=0, keepdims=True)

        total = lax.fori_loop(0, rows // TILE, powers, jnp.zeros((1, points), jnp.float32))
        inverse = 1.0 / total

        def add(r, carry):
            at = pl.ds(pl.multiple_of(r * TILE, TILE), TILE)
            weights = (logit[at, :] * inverse).astype(jnp.bfloat16)
            acc[at, :] += jnp.dot(weights, block(), preferred_element_type=jnp.float32)
            return carry

        lax.fori_loop(0, rows // TILE, add, 0)
        return carry

    lax.fori_loop(0, slots // GROUP, step, 0)

    def across(t, other_core):
        at = pl.ds(pl.multiple_of((2 * t + other_core) * share, share), share)
        return pltpu.make_async_remote_copy(
            src_ref=acc.at[at, :],
            dst_ref=pair.at[t],
            send_sem=pair_send.at[t],
            recv_sem=pair_recv.at[t],
            device_id=(me, partner),
            device_id_type=MESH,
        )

    def ring(d):
        return pltpu.make_async_remote_copy(
            src_ref=sbuf.at[d - 1],
            dst_ref=rbuf.at[d - 1],
            send_sem=ring_send.at[d - 1],
            recv_sem=ring_recv.at[d - 1],
            device_id=(me, ((chip + d) % chips) * 2 + core),
            device_id_type=MESH,
        )

    order = [2, 1, 3, 0][:chips]
    for d in order:
        across((chip + d) % chips, 1 - core).start()
    for d in order:
        t = (chip + d) % chips
        across(t, 1 - core).wait_recv()
        if d:
            at = pl.ds(pl.multiple_of((2 * t + core) * share, share), share)
            sbuf[d - 1] = (acc[at, :] + pair[t]).astype(jnp.bfloat16)
            ring(d).start()
    mine = pl.ds(pl.multiple_of(lane * share, share), share)
    value = acc[mine, :] + pair[chip] + cent_ref[mine, :].astype(jnp.float32)
    for d in order:
        if d:
            ring(d).wait_recv()
            value = value + rbuf[d - 1].astype(jnp.float32)
    scale = lax.rsqrt(jnp.mean(value * value, axis=-1, keepdims=True) + 1e-06)
    out_ref[...] = (value * scale).astype(jnp.bfloat16)

    def finish(q, carry):
        exchange(q).wait_send()
        return carry

    lax.fori_loop(1, slots, finish, 0)
    for d in order:
        across((chip + d) % chips, 1 - core).wait_send()
        if d:
            ring(d).wait_send()


def local(points, block_ids, block_counts, centroids):
    held, block_rows, feature = points.shape
    slots = lax.axis_size("cluster")
    copies = lax.axis_size("copy")
    rows = centroids.shape[0]
    share = rows // copies
    chips = copies // 2
    slot_index = jnp.arange(held, dtype=jnp.int32)
    matches = (block_ids[None, :] == jnp.arange(slots, dtype=jnp.int32)[:, None]) & (
        slot_index < block_counts[0]
    )[None, :]
    flag = jnp.any(matches, axis=1).astype(jnp.float32)
    position = jnp.sum(jnp.where(matches, slot_index[None, :], 0), axis=1).astype(jnp.int32)
    smem = pl.BlockSpec(memory_space=pltpu.SMEM)
    vmem = pl.BlockSpec(memory_space=pltpu.VMEM)
    blocks = (slots, block_rows, feature)
    dma = pltpu.SemaphoreType.DMA
    return pl.pallas_call(
        functools.partial(kernel, (slots, int(math.sqrt(slots)), copies)),
        out_shape=jax.ShapeDtypeStruct((share, feature), jnp.bfloat16),
        in_specs=[smem, smem, vmem, vmem],
        out_specs=vmem,
        scratch_shapes=[
            pltpu.VMEM(blocks, jnp.bfloat16),
            pltpu.VMEM(blocks, jnp.bfloat16),
            pltpu.VMEM((rows, GROUP * block_rows), jnp.float32),
            pltpu.VMEM((rows, feature), jnp.float32),
            pltpu.VMEM((chips, share, feature), jnp.float32),
            pltpu.VMEM((chips - 1, share, feature), jnp.bfloat16),
            pltpu.VMEM((chips - 1, share, feature), jnp.bfloat16),
            dma((slots,)),
            dma((slots,)),
            dma((chips,)),
            dma((chips,)),
            dma((chips - 1,)),
            dma((chips - 1,)),
        ],
        compiler_params=pltpu.CompilerParams(
            collective_id=0, has_side_effects=True, vmem_limit_bytes=56 << 20
        ),
    )(position, flag, points, centroids)


def solution(mesh):
    return jax.shard_map(
        local,
        mesh=mesh,
        in_specs=(
            P(("cluster", "copy"), None, None),
            P(("cluster", "copy")),
            P(("cluster", "copy")),
            P("cluster", None),
        ),
        out_specs=P(("cluster", "copy"), None),
        check_vma=False,
    )
```

```python
import functools
import math

import jax
import jax.numpy as jnp
from jax import lax
from jax.experimental import pallas as pl
from jax.experimental.pallas import tpu as pltpu
from jax.sharding import PartitionSpec as P

MESH = pl.DeviceIdType.MESH
GROUP = 4
LEAD = 2
BATCH = 8
TILE = 256


def kernel(
    shape, pos_ref, flag_ref, pts_ref, cent_ref, out_ref,
    stage, mid, recv, logit, acc, pair, sbuf, rbuf,
    send_sem, mid_sem, relay_sem, recv_sem, pair_send, pair_recv, ring_send, ring_recv,
):
    slots, side, copies = shape
    rows, feature = cent_ref.shape
    share = rows // copies
    chips = copies // 2
    me = lax.axis_index("cluster")
    lane = lax.axis_index("copy")
    row, col = me // side, me % side
    chip, core = lane // 2, lane % 2
    partner = chip * 2 + (1 - core)

    def ranked(a):
        return jnp.where(a % 2 == 0, 1 + a // 2, side - 1 - a // 2)

    def at_offset(dy, dz):
        return ((row + dy) % side) * side + (col + dz) % side

    def direct(q):
        d = ranked(q // 2)
        return jnp.where(q % 2 == 0, d, 0), jnp.where(q % 2 == 0, 0, d)

    def turning(r):
        dy = ranked(r % (side - 1))
        dz = ranked((r // (side - 1) + r) % (side - 1))
        return dy, dz, (dy + dz) % 2 == 0

    straight = 2 * (side - 1)
    relays = (side - 1) * (side - 1)

    barrier = pltpu.get_barrier_semaphore()

    def greet(q, carry):
        pl.semaphore_signal(
            barrier, inc=1, device_id=(at_offset(*direct(q)), lane), device_id_type=MESH
        )
        return carry

    lax.fori_loop(0, straight, greet, 0)
    pl.semaphore_signal(barrier, inc=1, device_id=(me, partner), device_id_type=MESH)
    for d in range(1, chips):
        other = ((chip + d) % chips) * 2 + core
        pl.semaphore_signal(barrier, inc=1, device_id=(me, other), device_id_type=MESH)

    recv[0] = pts_ref[pos_ref[me]] * flag_ref[me].astype(jnp.bfloat16)

    def fill(slot, k):
        stage[slot] = pts_ref[pos_ref[k]] * flag_ref[k].astype(jnp.bfloat16)

    def fill_straight(q, carry):
        fill(q, at_offset(*direct(q)))
        return carry

    def fill_turning(r, carry):
        dy, dz, _ = turning(r)
        fill(straight + r, at_offset(dy, dz))
        return carry

    lax.fori_loop(0, straight, fill_straight, 0)
    lax.fori_loop(0, relays, fill_turning, 0)
    acc[...] = jnp.zeros_like(acc)
    pl.semaphore_wait(barrier, straight + chips)

    def go(q):
        return pltpu.make_async_remote_copy(
            src_ref=stage.at[q],
            dst_ref=recv.at[1 + q],
            send_sem=send_sem.at[q],
            recv_sem=recv_sem.at[1 + q],
            device_id=(at_offset(*direct(q)), lane),
            device_id_type=MESH,
        )

    def first(r):
        dy, dz, along_y = turning(r)
        return pltpu.make_async_remote_copy(
            src_ref=stage.at[straight + r],
            dst_ref=mid.at[r],
            send_sem=send_sem.at[straight + r],
            recv_sem=mid_sem.at[r],
            device_id=(
                at_offset(jnp.where(along_y, dy, 0), jnp.where(along_y, 0, dz)), lane
            ),
            device_id_type=MESH,
        )

    def second(r):
        dy, dz, along_y = turning(r)
        return pltpu.make_async_remote_copy(
            src_ref=mid.at[r],
            dst_ref=recv.at[1 + straight + r],
            send_sem=relay_sem.at[r],
            recv_sem=recv_sem.at[1 + straight + r],
            device_id=(
                at_offset(jnp.where(along_y, 0, dy), jnp.where(along_y, dz, 0)), lane
            ),
            device_id_type=MESH,
        )

    def begin_straight(q, carry):
        go(q).start()
        return carry

    def begin_turning(r, carry):
        first(r).start()
        return carry

    def relay(r, carry):
        first(r).wait_recv()
        second(r).start()
        return carry

    lax.fori_loop(0, straight, begin_straight, 0)
    lax.fori_loop(0, relays, begin_turning, 0)

    alpha = 3.0 / math.sqrt(feature) * math.log2(math.e)
    points = GROUP * pts_ref.shape[1]

    def relayed(j):
        return jnp.clip((j - LEAD) * BATCH, 0, relays)

    def step(j, carry):
        lax.fori_loop(relayed(j), relayed(j + 1), relay, 0)

        def arrive(b, carry):
            slot = j * GROUP + b
            pltpu.make_async_copy(recv.at[slot], recv.at[slot], recv_sem.at[slot]).wait()
            return carry

        lax.fori_loop(jnp.where(j == 0, 1, 0), GROUP, arrive, 0)

        def block():
            return recv[pl.ds(j * GROUP, GROUP)].reshape(points, feature)

        def scores(r, top):
            at = pl.ds(pl.multiple_of(r * TILE, TILE), TILE)
            part = lax.dot_general(
                cent_ref[at, :], block(), (((1,), (1,)), ((), ())),
                preferred_element_type=jnp.float32,
            )
            logit[at, :] = part
            return jnp.maximum(top, jnp.max(part, axis=0, keepdims=True))

        top = lax.fori_loop(
            0, rows // TILE, scores, jnp.full((1, points), -jnp.inf, jnp.float32)
        ) * alpha

        def powers(r, total):
            at = pl.ds(pl.multiple_of(r * TILE, TILE), TILE)
            value = jnp.exp2(logit[at, :] * alpha - top)
            logit[at, :] = value
            return total + jnp.sum(value, axis=0, keepdims=True)

        total = lax.fori_loop(0, rows // TILE, powers, jnp.zeros((1, points), jnp.float32))
        inverse = 1.0 / total

        def add(r, carry):
            at = pl.ds(pl.multiple_of(r * TILE, TILE), TILE)
            weights = (logit[at, :] * inverse).astype(jnp.bfloat16)
            acc[at, :] += jnp.dot(weights, block(), preferred_element_type=jnp.float32)
            return carry

        lax.fori_loop(0, rows // TILE, add, 0)
        return carry

    lax.fori_loop(0, slots // GROUP, step, 0)

    def across(t, other_core):
        at = pl.ds(pl.multiple_of((2 * t + other_core) * share, share), share)
        return pltpu.make_async_remote_copy(
            src_ref=acc.at[at, :],
            dst_ref=pair.at[t],
            send_sem=pair_send.at[t],
            recv_sem=pair_recv.at[t],
            device_id=(me, partner),
            device_id_type=MESH,
        )

    def ring(d):
        return pltpu.make_async_remote_copy(
            src_ref=sbuf.at[d - 1],
            dst_ref=rbuf.at[d - 1],
            send_sem=ring_send.at[d - 1],
            recv_sem=ring_recv.at[d - 1],
            device_id=(me, ((chip + d) % chips) * 2 + core),
            device_id_type=MESH,
        )

    order = [2, 1, 3, 0][:chips]
    for d in order:
        across((chip + d) % chips, 1 - core).start()
    for d in order:
        t = (chip + d) % chips
        across(t, 1 - core).wait_recv()
        if d:
            at = pl.ds(pl.multiple_of((2 * t + core) * share, share), share)
            sbuf[d - 1] = (acc[at, :] + pair[t]).astype(jnp.bfloat16)
            ring(d).start()
    mine = pl.ds(pl.multiple_of(lane * share, share), share)
    value = acc[mine, :] + pair[chip] + cent_ref[mine, :].astype(jnp.float32)
    for d in order:
        if d:
            ring(d).wait_recv()
            value = value + rbuf[d - 1].astype(jnp.float32)
    scale = lax.rsqrt(jnp.mean(value * value, axis=-1, keepdims=True) + 1e-06)
    out_ref[...] = (value * scale).astype(jnp.bfloat16)

    def finish_straight(q, carry):
        go(q).wait_send()
        return carry

    def finish_turning(r, carry):
        first(r).wait_send()
        second(r).wait_send()
        return carry

    lax.fori_loop(0, straight, finish_straight, 0)
    lax.fori_loop(0, relays, finish_turning, 0)
    for d in order:
        across((chip + d) % chips, 1 - core).wait_send()
        if d:
            ring(d).wait_send()


def local(points, block_ids, block_counts, centroids):
    held, block_rows, feature = points.shape
    slots = lax.axis_size("cluster")
    copies = lax.axis_size("copy")
    rows = centroids.shape[0]
    share = rows // copies
    chips = copies // 2
    slot_index = jnp.arange(held, dtype=jnp.int32)
    matches = (block_ids[None, :] == jnp.arange(slots, dtype=jnp.int32)[:, None]) & (
        slot_index < block_counts[0]
    )[None, :]
    flag = jnp.any(matches, axis=1).astype(jnp.float32)
    position = jnp.sum(jnp.where(matches, slot_index[None, :], 0), axis=1).astype(jnp.int32)
    smem = pl.BlockSpec(memory_space=pltpu.SMEM)
    vmem = pl.BlockSpec(memory_space=pltpu.VMEM)
    side = int(math.sqrt(slots))
    relays = (side - 1) * (side - 1)
    blocks = (slots, block_rows, feature)
    dma = pltpu.SemaphoreType.DMA
    return pl.pallas_call(
        functools.partial(kernel, (slots, side, copies)),
        out_shape=jax.ShapeDtypeStruct((share, feature), jnp.bfloat16),
        in_specs=[smem, smem, vmem, vmem],
        out_specs=vmem,
        scratch_shapes=[
            pltpu.VMEM((slots - 1, block_rows, feature), jnp.bfloat16),
            pltpu.VMEM((relays, block_rows, feature), jnp.bfloat16),
            pltpu.VMEM(blocks, jnp.bfloat16),
            pltpu.VMEM((rows, GROUP * block_rows), jnp.float32),
            pltpu.VMEM((rows, feature), jnp.float32),
            pltpu.VMEM((chips, share, feature), jnp.float32),
            pltpu.VMEM((chips - 1, share, feature), jnp.bfloat16),
            pltpu.VMEM((chips - 1, share, feature), jnp.bfloat16),
            dma((slots - 1,)),
            dma((relays,)),
            dma((relays,)),
            dma((slots,)),
            dma((chips,)),
            dma((chips,)),
            dma((chips - 1,)),
            dma((chips - 1,)),
        ],
        compiler_params=pltpu.CompilerParams(
            collective_id=0, has_side_effects=True, vmem_limit_bytes=56 << 20
        ),
    )(position, flag, points, centroids)


def solution(mesh):
    return jax.shard_map(
        local,
        mesh=mesh,
        in_specs=(
            P(("cluster", "copy"), None, None),
            P(("cluster", "copy")),
            P(("cluster", "copy")),
            P("cluster", None),
        ),
        out_specs=P(("cluster", "copy"), None),
        check_vma=False,
    )
```

```python
import functools
import math

import jax
import jax.numpy as jnp
from jax import lax
from jax.experimental import pallas as pl
from jax.experimental.pallas import tpu as pltpu
from jax.sharding import PartitionSpec as P

MESH = pl.DeviceIdType.MESH
GROUP = 4
LEAD = 1
BATCH = 17
TILE = 512


def kernel(
    shape, ids_ref, count_ref, points_ref, centroids_ref, out_ref,
    pts_ref, cent_ref, stage, mid, recv, logit, acc, pair, sbuf, rbuf,
    send_sem, mid_sem, relay_sem, recv_sem, pair_send, pair_recv, ring_send, ring_recv, load_sem,
):
    slots, side, copies = shape
    rows, feature = cent_ref.shape
    share = rows // copies
    chips = copies // 2
    me = lax.axis_index("cluster")
    lane = lax.axis_index("copy")
    row, col = me // side, me % side
    chip, core = lane // 2, lane % 2
    partner = chip * 2 + (1 - core)

    def ranked(a):
        return jnp.where(a % 2 == 0, 1 + a // 2, side - 1 - a // 2)

    def at_offset(dy, dz):
        return ((row + dy) % side) * side + (col + dz) % side

    def direct(q):
        d = ranked(q // 2)
        return jnp.where(q % 2 == 0, d, 0), jnp.where(q % 2 == 0, 0, d)

    def turning(r):
        dy = ranked(r % (side - 1))
        dz = ranked((r // (side - 1) + r) % (side - 1))
        return dy, dz, (dy + dz) % 2 == 0

    straight = 2 * (side - 1)
    relays = (side - 1) * (side - 1)

    load_points = pltpu.make_async_copy(points_ref, pts_ref, load_sem.at[0])
    load_centroids = pltpu.make_async_copy(centroids_ref, cent_ref, load_sem.at[1])
    load_points.start()
    load_centroids.start()

    barrier = pltpu.get_barrier_semaphore()

    def greet(q, carry):
        pl.semaphore_signal(
            barrier, inc=1, device_id=(at_offset(*direct(q)), lane), device_id_type=MESH
        )
        return carry

    lax.fori_loop(0, straight, greet, 0)
    pl.semaphore_signal(barrier, inc=1, device_id=(me, partner), device_id_type=MESH)
    for d in range(1, chips):
        other = ((chip + d) % chips) * 2 + core
        pl.semaphore_signal(barrier, inc=1, device_id=(me, other), device_id_type=MESH)

    count = count_ref[0]
    held = pts_ref.shape[0]

    def routed(k):
        found = jnp.int32(0)
        where = jnp.int32(0)
        for n in range(held):
            hit = jnp.where(ids_ref[n] == k, 1, 0) * jnp.where(count > n, 1, 0)
            found = found + hit
            where = where + n * hit
        return pts_ref[where] * found.astype(jnp.float32).astype(jnp.bfloat16)

    load_points.wait()

    def fill_straight(q, carry):
        stage[q] = routed(at_offset(*direct(q)))
        return carry

    lax.fori_loop(0, straight, fill_straight, 0)
    pl.semaphore_wait(barrier, straight + chips)

    def go(q):
        return pltpu.make_async_remote_copy(
            src_ref=stage.at[q],
            dst_ref=recv.at[1 + q],
            send_sem=send_sem.at[q],
            recv_sem=recv_sem.at[1 + q],
            device_id=(at_offset(*direct(q)), lane),
            device_id_type=MESH,
        )

    def first(r):
        dy, dz, along_y = turning(r)
        return pltpu.make_async_remote_copy(
            src_ref=stage.at[straight + r],
            dst_ref=mid.at[r],
            send_sem=send_sem.at[straight + r],
            recv_sem=mid_sem.at[r],
            device_id=(
                at_offset(jnp.where(along_y, dy, 0), jnp.where(along_y, 0, dz)), lane
            ),
            device_id_type=MESH,
        )

    def second(r):
        dy, dz, along_y = turning(r)
        return pltpu.make_async_remote_copy(
            src_ref=mid.at[r],
            dst_ref=recv.at[1 + straight + r],
            send_sem=relay_sem.at[r],
            recv_sem=recv_sem.at[1 + straight + r],
            device_id=(
                at_offset(jnp.where(along_y, 0, dy), jnp.where(along_y, dz, 0)), lane
            ),
            device_id_type=MESH,
        )

    def begin_straight(q, carry):
        go(q).start()
        return carry

    def begin_turning(r, carry):
        dy, dz, _ = turning(r)
        stage[straight + r] = routed(at_offset(dy, dz))
        first(r).start()
        return carry

    def relay(r, carry):
        first(r).wait_recv()
        second(r).start()
        return carry

    lax.fori_loop(0, straight, begin_straight, 0)
    lax.fori_loop(0, relays, begin_turning, 0)
    recv[0] = routed(me)
    acc[...] = jnp.zeros_like(acc)
    load_centroids.wait()

    alpha = 3.0 / math.sqrt(feature) * math.log2(math.e)
    points = GROUP * pts_ref.shape[1]

    def relayed(j):
        return jnp.clip((j - LEAD) * BATCH, 0, relays)

    def ready(j):
        lax.fori_loop(relayed(j), relayed(j + 1), relay, 0)

        def arrive(b, carry):
            slot = j * GROUP + b
            pltpu.make_async_copy(recv.at[slot], recv.at[slot], recv_sem.at[slot]).wait()
            return carry

        lax.fori_loop(jnp.where(j == 0, 1, 0), GROUP, arrive, 0)

    def block(j):
        return recv[pl.ds(j * GROUP, GROUP)].reshape(points, feature)

    def tiles(function, initial):
        return lax.fori_loop(0, rows // TILE, function, initial, unroll=True)

    def exponentials(j):
        def scores(r, top):
            at = pl.ds(pl.multiple_of(r * TILE, TILE), TILE)
            part = lax.dot_general(
                cent_ref[at, :], block(j), (((1,), (1,)), ((), ())),
                preferred_element_type=jnp.float32,
            )
            logit[at, :] = part
            return jnp.maximum(top, jnp.max(part, axis=0, keepdims=True))

        top = tiles(scores, jnp.full((1, points), -jnp.inf, jnp.float32)) * alpha

        def powers(r, total):
            at = pl.ds(pl.multiple_of(r * TILE, TILE), TILE)
            value = jnp.exp2(logit[at, :] * alpha - top)
            logit[at, :] = value
            return total + jnp.sum(value, axis=0, keepdims=True)

        return 1.0 / tiles(powers, jnp.zeros((1, points), jnp.float32))

    def add(j, at, inverse):
        weights = (logit[at, :] * inverse).astype(jnp.bfloat16)
        acc[at, :] += jnp.dot(weights, block(j), preferred_element_type=jnp.float32)

    def step(j, carry):
        ready(j)
        inverse = exponentials(j)

        def sums(r, carry):
            add(j, pl.ds(pl.multiple_of(r * TILE, TILE), TILE), inverse)
            return carry

        tiles(sums, 0)
        return carry

    last = slots // GROUP - 1
    lax.fori_loop(0, last, step, 0)
    ready(last)
    inverse = exponentials(last)

    def across(t, other_core):
        at = pl.ds(pl.multiple_of((2 * t + other_core) * share, share), share)
        return pltpu.make_async_remote_copy(
            src_ref=acc.at[at, :],
            dst_ref=pair.at[t],
            send_sem=pair_send.at[t],
            recv_sem=pair_recv.at[t],
            device_id=(me, partner),
            device_id_type=MESH,
        )

    def ring(d):
        return pltpu.make_async_remote_copy(
            src_ref=sbuf.at[d - 1],
            dst_ref=rbuf.at[d - 1],
            send_sem=ring_send.at[d - 1],
            recv_sem=ring_recv.at[d - 1],
            device_id=(me, ((chip + d) % chips) * 2 + core),
            device_id_type=MESH,
        )

    def chunk(t, of_core):
        return pl.ds(pl.multiple_of((2 * t + of_core) * share, share), share)

    order = [2, 1, 3, 0][:chips]
    for d in order:
        t = (chip + d) % chips
        add(last, chunk(t, 1 - core), inverse)
        across(t, 1 - core).start()
    for d in order:
        t = (chip + d) % chips
        add(last, chunk(t, core), inverse)
        across(t, 1 - core).wait_recv()
        if d:
            sbuf[d - 1] = (acc[chunk(t, core), :] + pair[t]).astype(jnp.bfloat16)
            ring(d).start()
    mine = pl.ds(pl.multiple_of(lane * share, share), share)
    value = acc[mine, :] + pair[chip] + cent_ref[mine, :].astype(jnp.float32)
    for d in order:
        if d:
            ring(d).wait_recv()
            value = value + rbuf[d - 1].astype(jnp.float32)
    scale = lax.rsqrt(jnp.mean(value * value, axis=-1, keepdims=True) + 1e-06)
    out_ref[...] = (value * scale).astype(jnp.bfloat16)

    def finish_straight(q, carry):
        go(q).wait_send()
        return carry

    def finish_turning(r, carry):
        first(r).wait_send()
        second(r).wait_send()
        return carry

    lax.fori_loop(0, straight, finish_straight, 0)
    lax.fori_loop(0, relays, finish_turning, 0)
    for d in order:
        across((chip + d) % chips, 1 - core).wait_send()
        if d:
            ring(d).wait_send()


def local(points, block_ids, block_counts, centroids):
    held, block_rows, feature = points.shape
    slots = lax.axis_size("cluster")
    copies = lax.axis_size("copy")
    rows = centroids.shape[0]
    share = rows // copies
    chips = copies // 2
    smem = pl.BlockSpec(memory_space=pltpu.SMEM)
    anywhere = pl.BlockSpec(memory_space=pl.ANY)
    vmem = pl.BlockSpec(memory_space=pltpu.VMEM)
    side = int(math.sqrt(slots))
    relays = (side - 1) * (side - 1)
    blocks = (slots, block_rows, feature)
    dma = pltpu.SemaphoreType.DMA
    return pl.pallas_call(
        functools.partial(kernel, (slots, side, copies)),
        out_shape=jax.ShapeDtypeStruct((share, feature), jnp.bfloat16),
        in_specs=[smem, smem, anywhere, anywhere],
        out_specs=vmem,
        scratch_shapes=[
            pltpu.VMEM(points.shape, jnp.bfloat16),
            pltpu.VMEM(centroids.shape, jnp.bfloat16),
            pltpu.VMEM((slots - 1, block_rows, feature), jnp.bfloat16),
            pltpu.VMEM((relays, block_rows, feature), jnp.bfloat16),
            pltpu.VMEM(blocks, jnp.bfloat16),
            pltpu.VMEM((rows, GROUP * block_rows), jnp.float32),
            pltpu.VMEM((rows, feature), jnp.float32),
            pltpu.VMEM((chips, share, feature), jnp.float32),
            pltpu.VMEM((chips - 1, share, feature), jnp.bfloat16),
            pltpu.VMEM((chips - 1, share, feature), jnp.bfloat16),
            dma((slots - 1,)),
            dma((relays,)),
            dma((relays,)),
            dma((slots,)),
            dma((chips,)),
            dma((chips,)),
            dma((chips - 1,)),
            dma((chips - 1,)),
            dma((2,)),
        ],
        compiler_params=pltpu.CompilerParams(
            collective_id=0, has_side_effects=True, vmem_limit_bytes=56 << 20
        ),
    )(block_ids, block_counts, points, centroids)


def solution(mesh):
    return jax.shard_map(
        local,
        mesh=mesh,
        in_specs=(
            P(("cluster", "copy"), None, None),
            P(("cluster", "copy")),
            P(("cluster", "copy")),
            P("cluster", None),
        ),
        out_specs=P(("cluster", "copy"), None),
        check_vma=False,
    )
```

```python
import functools
import math

import jax
import jax.numpy as jnp
from jax import lax
from jax.experimental import pallas as pl
from jax.experimental.pallas import tpu as pltpu
from jax.sharding import PartitionSpec as P

MESH = pl.DeviceIdType.MESH
GROUP = 4
TILE = 512


def kernel(
    shape, ids_ref, count_ref, points_ref, centroids_ref, out_ref,
    pts_ref, cent_ref, raw1_up, raw1_down, raw2_up, raw2_down, picked, land3, land4,
    stage, recv, names, logit, acc, pair, sbuf, rbuf,
    near_send, near_recv, name_send, name_recv, far_send, far_recv,
    pair_send, pair_recv, ring_send, ring_recv, load_sem,
):
    slots, side, copies = shape
    rows, feature = cent_ref.shape
    held = pts_ref.shape[0]
    half = held // 2
    share = rows // copies
    chips = copies // 2
    me = lax.axis_index("cluster")
    lane = lax.axis_index("copy")
    chip, core = lane // 2, lane % 2
    partner = chip * 2 + (1 - core)
    u = (1 - core) * (me // side) + core * (me % side)
    v = (1 - core) * (me % side) + core * (me // side)

    def at_offset(du, dv):
        a, b = (u + du + side) % side, (v + dv + side) % side
        return (1 - core) * (a * side + b) + core * (b * side + a)

    def ranked(i):
        return jnp.where(i % 2 == 1, (i + 1) // 2, (side - i // 2) % side)

    load_points = pltpu.make_async_copy(points_ref, pts_ref, load_sem.at[0])
    load_centroids = pltpu.make_async_copy(centroids_ref, cent_ref, load_sem.at[1])
    load_points.start()
    load_centroids.start()

    barrier = pltpu.get_barrier_semaphore()

    def signal(cluster, copy):
        pl.semaphore_signal(barrier, inc=1, device_id=(cluster, copy), device_id_type=MESH)

    for d in (1, -1, 2, -2):
        signal(at_offset(d, 0), lane)

    def greet(d, carry):
        signal(at_offset(0, d), lane)
        return carry

    lax.fori_loop(1, side, greet, 0)
    signal(me, partner)
    for d in range(1, chips):
        signal(me, ((chip + d) % chips) * 2 + core)

    count = count_ref[0]
    column = lax.broadcasted_iota(jnp.int32, names.shape[1:], 1)
    listed = jnp.full(names.shape[1:], -1, jnp.int32)
    for n in range(held):
        listed = jnp.where(column == n, jnp.where(count > n, ids_ref[n], -1), listed)
    names[0] = listed

    def pick(source, entry, k):
        code = jnp.max(jnp.where(names[entry] == k, column + 1, 0))
        found = jnp.minimum(code, 1).astype(jnp.float32).astype(jnp.bfloat16)
        return source[jnp.maximum(code - 1, 0)] * found

    def send(src, dst, send_sem, recv_sem, cluster):
        return pltpu.make_async_remote_copy(
            src_ref=src,
            dst_ref=dst,
            send_sem=send_sem,
            recv_sem=recv_sem,
            device_id=(cluster, lane),
            device_id_type=MESH,
        )

    raw1, raw2 = (raw1_up, raw1_down), (raw2_up, raw2_down)
    sign = (1, -1)
    part = [pl.ds(0, half), pl.ds(half, half)]

    def tell(p, d):
        at = 2 * (d - 1) + p
        return send(
            names.at[0], names.at[1 + at], name_send.at[at], name_recv.at[at],
            at_offset(sign[p] * d, 0),
        )

    def hop1(p, h):
        return send(
            pts_ref.at[part[h]], raw1[p].at[part[h]],
            near_send.at[7 * p + h], near_recv.at[7 * p + h], at_offset(sign[p], 0),
        )

    def hop2(p, h):
        return send(
            raw1[p].at[part[h]], raw2[p].at[part[h]],
            near_send.at[7 * p + 2 + h], near_recv.at[7 * p + 2 + h], at_offset(sign[p], 0),
        )

    hop3_parts = [pl.ds(0, side // 2), pl.ds(side // 2, side)]

    def hop3(p, h):
        return send(
            picked.at[p, hop3_parts[h]], land3.at[p, hop3_parts[h]],
            near_send.at[7 * p + 4 + h], near_recv.at[7 * p + 4 + h], at_offset(sign[p], 0),
        )

    def hop4(p):
        return send(
            land3.at[p, hop3_parts[0]], land4.at[p],
            near_send.at[7 * p + 6], near_recv.at[7 * p + 6], at_offset(sign[p], 0),
        )

    sources = [pts_ref, raw1_up, raw1_down, raw2_up, raw2_down]

    def held_at(o, i):
        if o < 5:
            return stage.at[o, i]
        if o < 7:
            return land3.at[o - 5, side // 2 + i]
        return land4.at[i // (side // 2), i % (side // 2)]

    def across_v(o, i):
        return send(
            held_at(o, i), recv.at[o * side + i],
            far_send.at[o * side + i], far_recv.at[o * side + i], at_offset(0, ranked(i)),
        )

    def spread(o):
        def one(i, carry):
            if o < 5:
                stage[o, i] = pick(sources[o], o, at_offset(0, ranked(i)))
            across_v(o, i).start()
            return carry

        lax.fori_loop(1, side, one, 0)
        if o < 5:
            recv[o * side] = pick(sources[o], o, me)
        elif o < 7:
            recv[o * side] = land3[o - 5, side // 2]
        else:
            recv[o * side] = land4[0, 0]

    load_points.wait()
    pl.semaphore_wait(barrier, 4 + side - 1 + chips)
    both = (0, 1)
    for p in both:
        for d in (1, 2):
            tell(p, d).start()
    for h in both:
        for p in both:
            hop1(p, h).start()
    spread(0)
    acc[...] = jnp.zeros_like(acc)
    load_centroids.wait()

    def events(j):
        @pl.when(j == 0)
        def _():
            for p in both:
                hop1(p, 0).wait_recv()
                hop2(p, 0).start()

        @pl.when(j == 1)
        def _():
            for p in both:
                hop1(p, 1).wait_recv()
                hop2(p, 1).start()
            for p in both:
                tell(p, 1).wait_recv()
                spread(1 + p)

        @pl.when(j == 3)
        def _():
            for p in both:
                tell(p, 2).wait_recv()
                hop2(p, 0).wait_recv()
                hop2(p, 1).wait_recv()

                def beyond(i, carry):
                    k = at_offset(2 * sign[p], ranked(p * (side // 2) + i))
                    picked[p, i] = pick(raw2[p], 3 + p, k)
                    return carry

                def following(i, carry):
                    k = at_offset(sign[p], ranked(i))
                    picked[p, side // 2 + i] = pick(raw2[p], 3 + p, k)
                    return carry

                lax.fori_loop(0, side // 2, beyond, 0)
                hop3(p, 0).start()
                lax.fori_loop(0, side, following, 0)
                hop3(p, 1).start()
            for p in both:
                spread(3 + p)

        @pl.when(j == 6)
        def _():
            for p in both:
                hop3(p, 0).wait_recv()
                hop4(p).start()
            for p in both:
                hop3(p, 1).wait_recv()
                spread(5 + p)

        @pl.when(j == 8)
        def _():
            for p in both:
                hop4(p).wait_recv()
            spread(7)

    alpha = 3.0 / math.sqrt(feature) * math.log2(math.e)
    points = GROUP * pts_ref.shape[1]

    def ready(j):
        events(j)

        def arrive(b, carry):
            slot = j * GROUP + b
            pltpu.make_async_copy(recv.at[slot], recv.at[slot], far_recv.at[slot]).wait()
            return carry

        lax.fori_loop(jnp.where((j * GROUP) % side == 0, 1, 0), GROUP, arrive, 0)

    def block(j):
        return recv[pl.ds(j * GROUP, GROUP)].reshape(points, feature)

    def tiles(function, initial):
        return lax.fori_loop(0, rows // TILE, function, initial, unroll=True)

    def exponentials(j):
        def scores(r, top):
            at = pl.ds(pl.multiple_of(r * TILE, TILE), TILE)
            part = lax.dot_general(
                cent_ref[at, :], block(j), (((1,), (1,)), ((), ())),
                preferred_element_type=jnp.float32,
            )
            logit[at, :] = part
            return jnp.maximum(top, jnp.max(part, axis=0, keepdims=True))

        top = tiles(scores, jnp.full((1, points), -jnp.inf, jnp.float32)) * alpha

        def powers(r, total):
            at = pl.ds(pl.multiple_of(r * TILE, TILE), TILE)
            value = jnp.exp2(logit[at, :] * alpha - top)
            logit[at, :] = value
            return total + jnp.sum(value, axis=0, keepdims=True)

        return 1.0 / tiles(powers, jnp.zeros((1, points), jnp.float32))

    def add(j, at, inverse):
        weights = (logit[at, :] * inverse).astype(jnp.bfloat16)
        acc[at, :] += jnp.dot(weights, block(j), preferred_element_type=jnp.float32)

    def step(j, carry):
        ready(j)
        inverse = exponentials(j)

        def sums(r, carry):
            add(j, pl.ds(pl.multiple_of(r * TILE, TILE), TILE), inverse)
            return carry

        tiles(sums, 0)
        return carry

    last = slots // GROUP - 1
    lax.fori_loop(0, last, step, 0)
    ready(last)
    inverse = exponentials(last)

    def across(t, other_core):
        at = pl.ds(pl.multiple_of((2 * t + other_core) * share, share), share)
        return pltpu.make_async_remote_copy(
            src_ref=acc.at[at, :],
            dst_ref=pair.at[t],
            send_sem=pair_send.at[t],
            recv_sem=pair_recv.at[t],
            device_id=(me, partner),
            device_id_type=MESH,
        )

    def ring(d):
        return pltpu.make_async_remote_copy(
            src_ref=sbuf.at[d - 1],
            dst_ref=rbuf.at[d - 1],
            send_sem=ring_send.at[d - 1],
            recv_sem=ring_recv.at[d - 1],
            device_id=(me, ((chip + d) % chips) * 2 + core),
            device_id_type=MESH,
        )

    def chunk(t, of_core):
        return pl.ds(pl.multiple_of((2 * t + of_core) * share, share), share)

    order = [2, 1, 3, 0][:chips]
    for d in order:
        t = (chip + d) % chips
        add(last, chunk(t, 1 - core), inverse)
        across(t, 1 - core).start()
    for d in order:
        t = (chip + d) % chips
        add(last, chunk(t, core), inverse)
        across(t, 1 - core).wait_recv()
        if d:
            sbuf[d - 1] = (acc[chunk(t, core), :] + pair[t]).astype(jnp.bfloat16)
            ring(d).start()
    mine = pl.ds(pl.multiple_of(lane * share, share), share)
    value = acc[mine, :] + pair[chip] + cent_ref[mine, :].astype(jnp.float32)
    for d in order:
        if d:
            ring(d).wait_recv()
            value = value + rbuf[d - 1].astype(jnp.float32)
    scale = lax.rsqrt(jnp.mean(value * value, axis=-1, keepdims=True) + 1e-06)
    out_ref[...] = (value * scale).astype(jnp.bfloat16)

    for p in both:
        for h in both:
            tell(p, 1 + h).wait_send()
            hop1(p, h).wait_send()
            hop2(p, h).wait_send()
            hop3(p, h).wait_send()
        hop4(p).wait_send()
    for o in range(side):

        def sent(i, carry):
            across_v(o, i).wait_send()
            return carry

        lax.fori_loop(1, side, sent, 0)
    for d in order:
        across((chip + d) % chips, 1 - core).wait_send()
        if d:
            ring(d).wait_send()


def local(points, block_ids, block_counts, centroids):
    held, block_rows, feature = points.shape
    slots = lax.axis_size("cluster")
    copies = lax.axis_size("copy")
    rows = centroids.shape[0]
    share = rows // copies
    chips = copies // 2
    smem = pl.BlockSpec(memory_space=pltpu.SMEM)
    anywhere = pl.BlockSpec(memory_space=pl.ANY)
    vmem = pl.BlockSpec(memory_space=pltpu.VMEM)
    side = int(math.sqrt(slots))
    def blocks(*lead):
        return pltpu.VMEM((*lead, block_rows, feature), jnp.bfloat16)

    dma = pltpu.SemaphoreType.DMA
    return pl.pallas_call(
        functools.partial(kernel, (slots, side, copies)),
        out_shape=jax.ShapeDtypeStruct((share, feature), jnp.bfloat16),
        in_specs=[smem, smem, anywhere, anywhere],
        out_specs=vmem,
        scratch_shapes=[
            pltpu.VMEM(points.shape, jnp.bfloat16),
            pltpu.VMEM(centroids.shape, jnp.bfloat16),
            blocks(held),
            blocks(held),
            blocks(held),
            blocks(held),
            blocks(2, side + side // 2),
            blocks(2, side + side // 2),
            blocks(2, side // 2),
            blocks(5, side),
            blocks(slots),
            pltpu.VMEM((5, 8, 128), jnp.int32),
            pltpu.VMEM((rows, GROUP * block_rows), jnp.float32),
            pltpu.VMEM((rows, feature), jnp.float32),
            pltpu.VMEM((chips, share, feature), jnp.float32),
            pltpu.VMEM((chips - 1, share, feature), jnp.bfloat16),
            pltpu.VMEM((chips - 1, share, feature), jnp.bfloat16),
            dma((14,)),
            dma((14,)),
            dma((4,)),
            dma((4,)),
            dma((slots,)),
            dma((slots,)),
            dma((chips,)),
            dma((chips,)),
            dma((chips - 1,)),
            dma((chips - 1,)),
            dma((2,)),
        ],
        compiler_params=pltpu.CompilerParams(
            collective_id=0, has_side_effects=True, vmem_limit_bytes=56 << 20
        ),
    )(block_ids, block_counts, points, centroids)


def solution(mesh):
    return jax.shard_map(
        local,
        mesh=mesh,
        in_specs=(
            P(("cluster", "copy"), None, None),
            P(("cluster", "copy")),
            P(("cluster", "copy")),
            P("cluster", None),
        ),
        out_specs=P(("cluster", "copy"), None),
        check_vma=False,
    )
```

```python
import functools
import math

import jax
import jax.numpy as jnp
from jax import lax
from jax.experimental import pallas as pl
from jax.experimental.pallas import tpu as pltpu
from jax.sharding import PartitionSpec as P

MESH = pl.DeviceIdType.MESH
GROUP = 4
TILE = 512


def kernel(
    shape, ids_ref, count_ref, points_ref, centroids_ref, out_ref,
    pts_ref, cent_ref, raw1_up, raw1_down, raw2_up, raw2_down, picked, land3, land4,
    stage, recv, names, logit, acc, pair, sbuf, rbuf,
    near_send, near_recv, name_send, name_recv, far_send, far_recv,
    pair_send, pair_recv, ring_send, ring_recv, load_sem,
):
    slots, side, copies = shape
    rows, feature = cent_ref.shape
    held = pts_ref.shape[0]
    half = held // 2
    share = rows // copies
    chips = copies // 2
    me = lax.axis_index("cluster")
    lane = lax.axis_index("copy")
    chip, core = lane // 2, lane % 2
    partner = chip * 2 + (1 - core)
    u = (1 - core) * (me // side) + core * (me % side)
    v = (1 - core) * (me % side) + core * (me // side)

    def at_offset(du, dv):
        a, b = (u + du + side) % side, (v + dv + side) % side
        return (1 - core) * (a * side + b) + core * (b * side + a)

    def ranked(i):
        return jnp.where(i % 2 == 1, (i + 1) // 2, (side - i // 2) % side)

    load_points = pltpu.make_async_copy(points_ref, pts_ref, load_sem.at[0])
    load_centroids = pltpu.make_async_copy(centroids_ref, cent_ref, load_sem.at[1])
    load_points.start()
    load_centroids.start()

    barrier = pltpu.get_barrier_semaphore()

    def signal(cluster, copy):
        pl.semaphore_signal(barrier, inc=1, device_id=(cluster, copy), device_id_type=MESH)

    for d in (1, -1, 2, -2):
        signal(at_offset(d, 0), lane)

    def greet(d, carry):
        signal(at_offset(0, d), lane)
        return carry

    lax.fori_loop(1, side, greet, 0)
    signal(me, partner)
    for d in range(1, chips):
        signal(me, ((chip + d) % chips) * 2 + core)

    count = count_ref[0]
    column = lax.broadcasted_iota(jnp.int32, names.shape[1:], 1)
    listed = jnp.full(names.shape[1:], -1, jnp.int32)
    for n in range(held):
        listed = jnp.where(column == n, jnp.where(count > n, ids_ref[n], -1), listed)
    names[0] = listed

    def pick(source, entry, k):
        code = jnp.max(jnp.where(names[entry] == k, column + 1, 0))
        found = jnp.minimum(code, 1).astype(jnp.float32).astype(jnp.bfloat16)
        return source[jnp.maximum(code - 1, 0)] * found

    def send(src, dst, send_sem, recv_sem, cluster):
        return pltpu.make_async_remote_copy(
            src_ref=src,
            dst_ref=dst,
            send_sem=send_sem,
            recv_sem=recv_sem,
            device_id=(cluster, lane),
            device_id_type=MESH,
        )

    raw1, raw2 = (raw1_up, raw1_down), (raw2_up, raw2_down)
    sign = (1, -1)
    part = [pl.ds(0, half), pl.ds(half, half)]

    def tell(p, d):
        at = 2 * (d - 1) + p
        return send(
            names.at[0], names.at[1 + at], name_send.at[at], name_recv.at[at],
            at_offset(sign[p] * d, 0),
        )

    def hop1(p, h):
        return send(
            pts_ref.at[part[h]], raw1[p].at[part[h]],
            near_send.at[7 * p + h], near_recv.at[7 * p + h], at_offset(sign[p], 0),
        )

    def hop2(p, h):
        return send(
            raw1[p].at[part[h]], raw2[p].at[part[h]],
            near_send.at[7 * p + 2 + h], near_recv.at[7 * p + 2 + h], at_offset(sign[p], 0),
        )

    hop3_parts = [pl.ds(0, side // 2), pl.ds(side // 2, side)]

    def hop3(p, h):
        return send(
            picked.at[p, hop3_parts[h]], land3.at[p, hop3_parts[h]],
            near_send.at[7 * p + 4 + h], near_recv.at[7 * p + 4 + h], at_offset(sign[p], 0),
        )

    def hop4(p):
        return send(
            land3.at[p, hop3_parts[0]], land4.at[p],
            near_send.at[7 * p + 6], near_recv.at[7 * p + 6], at_offset(sign[p], 0),
        )

    sources = [pts_ref, raw1_up, raw1_down, raw2_up, raw2_down]

    def held_at(o, i):
        if o < 5:
            return stage.at[o, i]
        if o < 7:
            return land3.at[o - 5, side // 2 + i]
        return land4.at[i // (side // 2), i % (side // 2)]

    def across_v(o, i):
        return send(
            held_at(o, i), recv.at[o * side + i],
            far_send.at[o * side + i], far_recv.at[o * side + i], at_offset(0, ranked(i)),
        )

    def spread(o):
        def one(i, carry):
            if o < 5:
                stage[o, i] = pick(sources[o], o, at_offset(0, ranked(i)))
            across_v(o, i).start()
            return carry

        lax.fori_loop(1, side, one, 0)
        if o < 5:
            recv[o * side] = pick(sources[o], o, me)
        elif o < 7:
            recv[o * side] = land3[o - 5, side // 2]
        else:
            recv[o * side] = land4[0, 0]

    load_points.wait()
    pl.semaphore_wait(barrier, 4 + side - 1 + chips)
    both = (0, 1)
    for p in both:
        for d in (1, 2):
            tell(p, d).start()
    for h in both:
        for p in both:
            hop1(p, h).start()
    acc[...] = jnp.zeros_like(acc)
    load_centroids.wait()
    for h in both:
        for p in both:
            hop1(p, h).wait_recv()
            hop2(p, h).start()
    for p in both:
        tell(p, 2).wait_recv()
        hop2(p, 0).wait_recv()
        hop2(p, 1).wait_recv()

        def beyond(i, carry):
            k = at_offset(2 * sign[p], ranked(p * (side // 2) + i))
            picked[p, i] = pick(raw2[p], 3 + p, k)
            return carry

        def following(i, carry):
            k = at_offset(sign[p], ranked(i))
            picked[p, side // 2 + i] = pick(raw2[p], 3 + p, k)
            return carry

        lax.fori_loop(0, side // 2, beyond, 0)
        hop3(p, 0).start()
        lax.fori_loop(0, side, following, 0)
        hop3(p, 1).start()
    for p in both:
        hop3(p, 0).wait_recv()
        hop4(p).start()
    for p in both:
        tell(p, 1).wait_recv()
        hop3(p, 1).wait_recv()
    spread(0)
    spread(1)
    for p in both:
        hop4(p).wait_recv()
    for o in range(2, side):
        spread(o)

    alpha = 3.0 / math.sqrt(feature) * math.log2(math.e)
    points = GROUP * pts_ref.shape[1]

    def ready(j):
        def arrive(b, carry):
            slot = j * GROUP + b
            pltpu.make_async_copy(recv.at[slot], recv.at[slot], far_recv.at[slot]).wait()
            return carry

        lax.fori_loop(jnp.where((j * GROUP) % side == 0, 1, 0), GROUP, arrive, 0)

    def block(j):
        return recv[pl.ds(j * GROUP, GROUP)].reshape(points, feature)

    def tiles(function, initial):
        return lax.fori_loop(0, rows // TILE, function, initial, unroll=True)

    def exponentials(j):
        def scores(r, top):
            at = pl.ds(pl.multiple_of(r * TILE, TILE), TILE)
            part = lax.dot_general(
                cent_ref[at, :], block(j), (((1,), (1,)), ((), ())),
                preferred_element_type=jnp.float32,
            )
            logit[at, :] = part
            return jnp.maximum(top, jnp.max(part, axis=0, keepdims=True))

        top = tiles(scores, jnp.full((1, points), -jnp.inf, jnp.float32)) * alpha

        def powers(r, total):
            at = pl.ds(pl.multiple_of(r * TILE, TILE), TILE)
            value = jnp.exp2(logit[at, :] * alpha - top)
            logit[at, :] = value
            return total + jnp.sum(value, axis=0, keepdims=True)

        return 1.0 / tiles(powers, jnp.zeros((1, points), jnp.float32))

    def add(j, at, inverse):
        weights = (logit[at, :] * inverse).astype(jnp.bfloat16)
        acc[at, :] += jnp.dot(weights, block(j), preferred_element_type=jnp.float32)

    def step(j, carry):
        ready(j)
        inverse = exponentials(j)

        def sums(r, carry):
            add(j, pl.ds(pl.multiple_of(r * TILE, TILE), TILE), inverse)
            return carry

        tiles(sums, 0)
        return carry

    last = slots // GROUP - 1
    lax.fori_loop(0, last, step, 0)
    ready(last)
    inverse = exponentials(last)

    def across(t, other_core):
        at = pl.ds(pl.multiple_of((2 * t + other_core) * share, share), share)
        return pltpu.make_async_remote_copy(
            src_ref=acc.at[at, :],
            dst_ref=pair.at[t],
            send_sem=pair_send.at[t],
            recv_sem=pair_recv.at[t],
            device_id=(me, partner),
            device_id_type=MESH,
        )

    def ring(d):
        return pltpu.make_async_remote_copy(
            src_ref=sbuf.at[d - 1],
            dst_ref=rbuf.at[d - 1],
            send_sem=ring_send.at[d - 1],
            recv_sem=ring_recv.at[d - 1],
            device_id=(me, ((chip + d) % chips) * 2 + core),
            device_id_type=MESH,
        )

    def chunk(t, of_core):
        return pl.ds(pl.multiple_of((2 * t + of_core) * share, share), share)

    order = [2, 1, 3, 0][:chips]
    for d in order:
        t = (chip + d) % chips
        add(last, chunk(t, 1 - core), inverse)
        across(t, 1 - core).start()
    for d in order:
        t = (chip + d) % chips
        add(last, chunk(t, core), inverse)
        across(t, 1 - core).wait_recv()
        if d:
            sbuf[d - 1] = (acc[chunk(t, core), :] + pair[t]).astype(jnp.bfloat16)
            ring(d).start()
    for p in both:
        for h in both:
            tell(p, 1 + h).wait_send()
            hop1(p, h).wait_send()
            hop2(p, h).wait_send()
            hop3(p, h).wait_send()
        hop4(p).wait_send()
    for o in range(side):

        def sent(i, carry):
            across_v(o, i).wait_send()
            return carry

        lax.fori_loop(1, side, sent, 0)
    for d in order:
        across((chip + d) % chips, 1 - core).wait_send()
    mine = pl.ds(pl.multiple_of(lane * share, share), share)
    value = acc[mine, :] + pair[chip] + cent_ref[mine, :].astype(jnp.float32)
    for d in order:
        if d:
            ring(d).wait_recv()
            value = value + rbuf[d - 1].astype(jnp.float32)
    scale = lax.rsqrt(jnp.mean(value * value, axis=-1, keepdims=True) + 1e-06)
    out_ref[...] = (value * scale).astype(jnp.bfloat16)

    for d in order:
        if d:
            ring(d).wait_send()


def local(points, block_ids, block_counts, centroids):
    held, block_rows, feature = points.shape
    slots = lax.axis_size("cluster")
    copies = lax.axis_size("copy")
    rows = centroids.shape[0]
    share = rows // copies
    chips = copies // 2
    smem = pl.BlockSpec(memory_space=pltpu.SMEM)
    anywhere = pl.BlockSpec(memory_space=pl.ANY)
    vmem = pl.BlockSpec(memory_space=pltpu.VMEM)
    side = int(math.sqrt(slots))
    def blocks(*lead):
        return pltpu.VMEM((*lead, block_rows, feature), jnp.bfloat16)

    dma = pltpu.SemaphoreType.DMA
    return pl.pallas_call(
        functools.partial(kernel, (slots, side, copies)),
        out_shape=jax.ShapeDtypeStruct((share, feature), jnp.bfloat16),
        in_specs=[smem, smem, anywhere, anywhere],
        out_specs=vmem,
        scratch_shapes=[
            pltpu.VMEM(points.shape, jnp.bfloat16),
            pltpu.VMEM(centroids.shape, jnp.bfloat16),
            blocks(held),
            blocks(held),
            blocks(held),
            blocks(held),
            blocks(2, side + side // 2),
            blocks(2, side + side // 2),
            blocks(2, side // 2),
            blocks(5, side),
            blocks(slots),
            pltpu.VMEM((5, 8, 128), jnp.int32),
            pltpu.VMEM((rows, GROUP * block_rows), jnp.float32),
            pltpu.VMEM((rows, feature), jnp.float32),
            pltpu.VMEM((chips, share, feature), jnp.float32),
            pltpu.VMEM((chips - 1, share, feature), jnp.bfloat16),
            pltpu.VMEM((chips - 1, share, feature), jnp.bfloat16),
            dma((14,)),
            dma((14,)),
            dma((4,)),
            dma((4,)),
            dma((slots,)),
            dma((slots,)),
            dma((chips,)),
            dma((chips,)),
            dma((chips - 1,)),
            dma((chips - 1,)),
            dma((2,)),
        ],
        compiler_params=pltpu.CompilerParams(
            collective_id=0, has_side_effects=True, vmem_limit_bytes=56 << 20
        ),
    )(block_ids, block_counts, points, centroids)


def solution(mesh):
    return jax.shard_map(
        local,
        mesh=mesh,
        in_specs=(
            P(("cluster", "copy"), None, None),
            P(("cluster", "copy")),
            P(("cluster", "copy")),
            P("cluster", None),
        ),
        out_specs=P(("cluster", "copy"), None),
        check_vma=False,
    )
```

```python
import functools
import math

import jax
import jax.numpy as jnp
from jax import lax
from jax.experimental import pallas as pl
from jax.experimental.pallas import tpu as pltpu
from jax.sharding import PartitionSpec as P

MESH = pl.DeviceIdType.MESH
GROUP = 4
TILE = 512


def kernel(
    shape, ids_ref, count_ref, points_ref, centroids_ref, out_ref,
    pts_ref, cent_ref, raw1_up, raw1_down, raw2_up, raw2_down, picked, land3, land4,
    stage, recv, names, logit, acc, pair, sbuf, rbuf,
    near_send, near_recv, name_send, name_recv, far_send, far_recv,
    pair_send, pair_recv, ring_send, ring_recv, load_sem,
):
    slots, side, copies = shape
    rows, feature = cent_ref.shape
    held = pts_ref.shape[0]
    half = held // 2
    share = rows // copies
    chips = copies // 2
    me = lax.axis_index("cluster")
    lane = lax.axis_index("copy")
    chip, core = lane // 2, lane % 2
    partner = chip * 2 + (1 - core)
    u = (1 - core) * (me // side) + core * (me % side)
    v = (1 - core) * (me % side) + core * (me // side)

    def at_offset(du, dv):
        a, b = (u + du + side) % side, (v + dv + side) % side
        return (1 - core) * (a * side + b) + core * (b * side + a)

    def ranked(i):
        return jnp.where(i % 2 == 1, (i + 1) // 2, (side - i // 2) % side)

    load_points = pltpu.make_async_copy(points_ref, pts_ref, load_sem.at[0])
    load_centroids = pltpu.make_async_copy(centroids_ref, cent_ref, load_sem.at[1])
    load_points.start()
    load_centroids.start()

    barrier = pltpu.get_barrier_semaphore()

    def signal(cluster, copy):
        pl.semaphore_signal(barrier, inc=1, device_id=(cluster, copy), device_id_type=MESH)

    for d in (1, -1, 2, -2):
        signal(at_offset(d, 0), lane)

    def greet(d, carry):
        signal(at_offset(0, d), lane)
        return carry

    lax.fori_loop(1, side, greet, 0)
    signal(me, partner)
    for d in range(1, chips):
        signal(me, ((chip + d) % chips) * 2 + core)

    count = count_ref[0]
    column = lax.broadcasted_iota(jnp.int32, names.shape[1:], 1)
    listed = jnp.full(names.shape[1:], -1, jnp.int32)
    for n in range(held):
        listed = jnp.where(column == n, jnp.where(count > n, ids_ref[n], -1), listed)
    names[0] = listed

    def pick(source, entry, k):
        code = jnp.max(jnp.where(names[entry] == k, column + 1, 0))
        found = jnp.minimum(code, 1).astype(jnp.float32).astype(jnp.bfloat16)
        return source[jnp.maximum(code - 1, 0)] * found

    def send(src, dst, send_sem, recv_sem, cluster):
        return pltpu.make_async_remote_copy(
            src_ref=src,
            dst_ref=dst,
            send_sem=send_sem,
            recv_sem=recv_sem,
            device_id=(cluster, lane),
            device_id_type=MESH,
        )

    raw1, raw2 = (raw1_up, raw1_down), (raw2_up, raw2_down)
    sign = (1, -1)
    part = [pl.ds(0, half), pl.ds(half, half)]

    def tell(p, d):
        at = 2 * (d - 1) + p
        return send(
            names.at[0], names.at[1 + at], name_send.at[at], name_recv.at[at],
            at_offset(sign[p] * d, 0),
        )

    def hop1(p, h):
        return send(
            points_ref.at[part[h]], raw1[p].at[part[h]],
            near_send.at[7 * p + h], near_recv.at[7 * p + h], at_offset(sign[p], 0),
        )

    def hop2(p, h):
        return send(
            raw1[p].at[part[h]], raw2[p].at[part[h]],
            near_send.at[7 * p + 2 + h], near_recv.at[7 * p + 2 + h], at_offset(sign[p], 0),
        )

    hop3_parts = [pl.ds(0, side // 2), pl.ds(side // 2, side)]

    def hop3(p, h):
        return send(
            picked.at[p, hop3_parts[h]], land3.at[p, hop3_parts[h]],
            near_send.at[7 * p + 4 + h], near_recv.at[7 * p + 4 + h], at_offset(sign[p], 0),
        )

    def hop4(p):
        return send(
            land3.at[p, hop3_parts[0]], land4.at[p],
            near_send.at[7 * p + 6], near_recv.at[7 * p + 6], at_offset(sign[p], 0),
        )

    sources = [pts_ref, raw1_up, raw1_down, raw2_up, raw2_down]

    def held_at(o, i):
        if o < 5:
            return stage.at[o, i]
        if o < 7:
            return land3.at[o - 5, side // 2 + i]
        return land4.at[i // (side // 2), i % (side // 2)]

    def across_v(o, i):
        return send(
            held_at(o, i), recv.at[o * side + i],
            far_send.at[o * side + i], far_recv.at[o * side + i], at_offset(0, ranked(i)),
        )

    def prepare(o):
        def one(i, carry):
            stage[o, i] = pick(sources[o], o, at_offset(0, ranked(i)))
            return carry

        lax.fori_loop(1, side, one, 0)
        recv[o * side] = pick(sources[o], o, me)

    def spread(o, start=1):
        def one(i, carry):
            across_v(o, i).start()
            return carry

        lax.fori_loop(start, side, one, 0)
        if o in (5, 6):
            recv[o * side] = land3[o - 5, side // 2]
        elif o == 7:
            recv[o * side] = land4[0, 0]

    pl.semaphore_wait(barrier, 4 + side - 1 + chips)
    both = (0, 1)
    for h in both:
        for p in both:
            hop1(p, h).start()
    for p in both:
        for d in (1, 2):
            tell(p, d).start()
    load_points.wait()
    prepare(0)
    acc[...] = jnp.zeros_like(acc)
    load_centroids.wait()
    for h in both:
        for p in both:
            hop1(p, h).wait_recv()
            hop2(p, h).start()
    for p in both:
        tell(p, 1).wait_recv()
        prepare(1 + p)
    for p in both:
        tell(p, 2).wait_recv()
        hop2(p, 0).wait_recv()
        hop2(p, 1).wait_recv()

    fillers = 2
    for i in range(1, 1 + fillers):
        across_v(0, i).start()

    for p in both:

        def beyond(i, carry):
            k = at_offset(2 * sign[p], ranked(p * (side // 2) + i))
            picked[p, i] = pick(raw2[p], 3 + p, k)
            return carry

        lax.fori_loop(0, side // 2, beyond, 0)
        hop3(p, 0).start()
    for p in both:

        def following(i, carry):
            k = at_offset(sign[p], ranked(i))
            picked[p, side // 2 + i] = pick(raw2[p], 3 + p, k)
            return carry

        lax.fori_loop(0, side, following, 0)
        hop3(p, 1).start()
    for p in both:
        prepare(3 + p)
    for p in both:
        hop3(p, 0).wait_recv()
        hop4(p).start()
    for p in both:
        hop3(p, 1).wait_recv()
    spread(0, 1 + fillers)
    spread(1)
    for p in both:
        hop4(p).wait_recv()
    for o in range(2, side):
        spread(o)

    alpha = 3.0 / math.sqrt(feature) * math.log2(math.e)
    points = GROUP * pts_ref.shape[1]

    def ready(j):
        def arrive(b, carry):
            slot = j * GROUP + b
            pltpu.make_async_copy(recv.at[slot], recv.at[slot], far_recv.at[slot]).wait()
            return carry

        lax.fori_loop(jnp.where((j * GROUP) % side == 0, 1, 0), GROUP, arrive, 0)

    def block(j):
        return recv[pl.ds(j * GROUP, GROUP)].reshape(points, feature)

    def tiles(function, initial):
        return lax.fori_loop(0, rows // TILE, function, initial, unroll=True)

    def exponentials(j):
        def scores(r, top):
            at = pl.ds(pl.multiple_of(r * TILE, TILE), TILE)
            part = lax.dot_general(
                cent_ref[at, :], block(j), (((1,), (1,)), ((), ())),
                preferred_element_type=jnp.float32,
            )
            logit[at, :] = part
            return jnp.maximum(top, jnp.max(part, axis=0, keepdims=True))

        top = tiles(scores, jnp.full((1, points), -jnp.inf, jnp.float32)) * alpha

        def powers(r, total):
            at = pl.ds(pl.multiple_of(r * TILE, TILE), TILE)
            value = jnp.exp2(logit[at, :] * alpha - top)
            logit[at, :] = value
            return total + jnp.sum(value, axis=0, keepdims=True)

        return 1.0 / tiles(powers, jnp.zeros((1, points), jnp.float32))

    def add(j, at, inverse):
        weights = (logit[at, :] * inverse).astype(jnp.bfloat16)
        acc[at, :] += jnp.dot(weights, block(j), preferred_element_type=jnp.float32)

    def step(j, carry):
        ready(j)
        inverse = exponentials(j)

        def sums(r, carry):
            add(j, pl.ds(pl.multiple_of(r * TILE, TILE), TILE), inverse)
            return carry

        tiles(sums, 0)
        return carry

    last = slots // GROUP - 1
    lax.fori_loop(0, last, step, 0)
    ready(last)
    inverse = exponentials(last)

    def across(t, other_core):
        at = pl.ds(pl.multiple_of((2 * t + other_core) * share, share), share)
        return pltpu.make_async_remote_copy(
            src_ref=acc.at[at, :],
            dst_ref=pair.at[t],
            send_sem=pair_send.at[t],
            recv_sem=pair_recv.at[t],
            device_id=(me, partner),
            device_id_type=MESH,
        )

    def ring(d):
        return pltpu.make_async_remote_copy(
            src_ref=sbuf.at[d - 1],
            dst_ref=rbuf.at[d - 1],
            send_sem=ring_send.at[d - 1],
            recv_sem=ring_recv.at[d - 1],
            device_id=(me, ((chip + d) % chips) * 2 + core),
            device_id_type=MESH,
        )

    def chunk(t, of_core):
        return pl.ds(pl.multiple_of((2 * t + of_core) * share, share), share)

    order = [2, 1, 3, 0][:chips]
    for d in order:
        t = (chip + d) % chips
        add(last, chunk(t, 1 - core), inverse)
        across(t, 1 - core).start()
    for d in order:
        t = (chip + d) % chips
        add(last, chunk(t, core), inverse)
        across(t, 1 - core).wait_recv()
        if d:
            sbuf[d - 1] = (acc[chunk(t, core), :] + pair[t]).astype(jnp.bfloat16)
            ring(d).start()
    for p in both:
        for h in both:
            tell(p, 1 + h).wait_send()
            hop1(p, h).wait_send()
            hop2(p, h).wait_send()
            hop3(p, h).wait_send()
        hop4(p).wait_send()
    for o in range(side):

        def sent(i, carry):
            across_v(o, i).wait_send()
            return carry

        lax.fori_loop(1, side, sent, 0)
    for d in order:
        across((chip + d) % chips, 1 - core).wait_send()
    mine = pl.ds(pl.multiple_of(lane * share, share), share)
    value = acc[mine, :] + pair[chip] + cent_ref[mine, :].astype(jnp.float32)
    for d in order:
        if d:
            ring(d).wait_recv()
            value = value + rbuf[d - 1].astype(jnp.float32)
    scale = lax.rsqrt(jnp.mean(value * value, axis=-1, keepdims=True) + 1e-06)
    out_ref[...] = (value * scale).astype(jnp.bfloat16)

    for d in order:
        if d:
            ring(d).wait_send()


def local(points, block_ids, block_counts, centroids):
    held, block_rows, feature = points.shape
    slots = lax.axis_size("cluster")
    copies = lax.axis_size("copy")
    rows = centroids.shape[0]
    share = rows // copies
    chips = copies // 2
    smem = pl.BlockSpec(memory_space=pltpu.SMEM)
    anywhere = pl.BlockSpec(memory_space=pl.ANY)
    vmem = pl.BlockSpec(memory_space=pltpu.VMEM)
    side = int(math.sqrt(slots))
    def blocks(*lead):
        return pltpu.VMEM((*lead, block_rows, feature), jnp.bfloat16)

    dma = pltpu.SemaphoreType.DMA
    return pl.pallas_call(
        functools.partial(kernel, (slots, side, copies)),
        out_shape=jax.ShapeDtypeStruct((share, feature), jnp.bfloat16),
        in_specs=[smem, smem, anywhere, anywhere],
        out_specs=vmem,
        scratch_shapes=[
            pltpu.VMEM(points.shape, jnp.bfloat16),
            pltpu.VMEM(centroids.shape, jnp.bfloat16),
            blocks(held),
            blocks(held),
            blocks(held),
            blocks(held),
            blocks(2, side + side // 2),
            blocks(2, side + side // 2),
            blocks(2, side // 2),
            blocks(5, side),
            blocks(slots),
            pltpu.VMEM((5, 8, 128), jnp.int32),
            pltpu.VMEM((rows, GROUP * block_rows), jnp.float32),
            pltpu.VMEM((rows, feature), jnp.float32),
            pltpu.VMEM((chips, share, feature), jnp.float32),
            pltpu.VMEM((chips - 1, share, feature), jnp.bfloat16),
            pltpu.VMEM((chips - 1, share, feature), jnp.bfloat16),
            dma((14,)),
            dma((14,)),
            dma((4,)),
            dma((4,)),
            dma((slots,)),
            dma((slots,)),
            dma((chips,)),
            dma((chips,)),
            dma((chips - 1,)),
            dma((chips - 1,)),
            dma((2,)),
        ],
        compiler_params=pltpu.CompilerParams(
            collective_id=0, has_side_effects=True, vmem_limit_bytes=56 << 20
        ),
    )(block_ids, block_counts, points, centroids)


def solution(mesh):
    return jax.shard_map(
        local,
        mesh=mesh,
        in_specs=(
            P(("cluster", "copy"), None, None),
            P(("cluster", "copy")),
            P(("cluster", "copy")),
            P("cluster", None),
        ),
        out_specs=P(("cluster", "copy"), None),
        check_vma=False,
    )
```

```python
import functools
import math

import jax
import jax.numpy as jnp
from jax import lax
from jax.experimental import pallas as pl
from jax.experimental.pallas import tpu as pltpu
from jax.sharding import PartitionSpec as P

MESH = pl.DeviceIdType.MESH
GROUP = 4
TILE = 512


def kernel(
    shape, ids_ref, count_ref, points_ref, centroids_ref, out_ref,
    pts_ref, cent_ref, raw1_up, raw1_down, raw2_up, raw2_down, picked, land3, land4,
    stage, recv, names, logit, acc, pair, sbuf, rbuf,
    near_send, near_recv, name_send, name_recv, far_send, far_recv,
    pair_send, pair_recv, ring_send, ring_recv, load_sem,
):
    slots, side, copies = shape
    rows, feature = cent_ref.shape
    held = pts_ref.shape[0]
    half = held // 2
    share = rows // copies
    chips = copies // 2
    me = lax.axis_index("cluster")
    lane = lax.axis_index("copy")
    chip, core = lane // 2, lane % 2
    partner = chip * 2 + (1 - core)
    u = (1 - core) * (me // side) + core * (me % side)
    v = (1 - core) * (me % side) + core * (me // side)

    def at_offset(du, dv):
        a, b = (u + du + side) % side, (v + dv + side) % side
        return (1 - core) * (a * side + b) + core * (b * side + a)

    def ranked(i):
        far = jnp.where(i % 2 == 1, side // 2 - i // 2, side // 2 + i // 2)
        return jnp.where(i == 0, 0, far)

    load_points = pltpu.make_async_copy(points_ref, pts_ref, load_sem.at[0])
    load_centroids = pltpu.make_async_copy(centroids_ref, cent_ref, load_sem.at[1])
    load_points.start()
    load_centroids.start()

    barrier = pltpu.get_barrier_semaphore()

    def signal(cluster, copy):
        pl.semaphore_signal(barrier, inc=1, device_id=(cluster, copy), device_id_type=MESH)

    for d in (1, -1, 2, -2):
        signal(at_offset(d, 0), lane)

    def greet(d, carry):
        signal(at_offset(0, d), lane)
        return carry

    lax.fori_loop(1, side, greet, 0)
    signal(me, partner)
    for d in range(1, chips):
        signal(me, ((chip + d) % chips) * 2 + core)

    count = count_ref[0]
    column = lax.broadcasted_iota(jnp.int32, names.shape[1:], 1)
    listed = jnp.full(names.shape[1:], -1, jnp.int32)
    for n in range(held):
        listed = jnp.where(column == n, jnp.where(count > n, ids_ref[n], -1), listed)
    names[0] = listed

    def pick(source, entry, k):
        code = jnp.max(jnp.where(names[entry] == k, column + 1, 0))
        found = jnp.minimum(code, 1).astype(jnp.float32).astype(jnp.bfloat16)
        return source[jnp.maximum(code - 1, 0)] * found

    def send(src, dst, send_sem, recv_sem, cluster):
        return pltpu.make_async_remote_copy(
            src_ref=src,
            dst_ref=dst,
            send_sem=send_sem,
            recv_sem=recv_sem,
            device_id=(cluster, lane),
            device_id_type=MESH,
        )

    raw1, raw2 = (raw1_up, raw1_down), (raw2_up, raw2_down)
    sign = (1, -1)
    part = [pl.ds(0, half), pl.ds(half, half)]

    def tell(p, d):
        at = 2 * (d - 1) + p
        return send(
            names.at[0], names.at[1 + at], name_send.at[at], name_recv.at[at],
            at_offset(sign[p] * d, 0),
        )

    def hop1(p, h):
        return send(
            points_ref.at[part[h]], raw1[p].at[part[h]],
            near_send.at[7 * p + h], near_recv.at[7 * p + h], at_offset(sign[p], 0),
        )

    def hop2(p, h):
        return send(
            raw1[p].at[part[h]], raw2[p].at[part[h]],
            near_send.at[7 * p + 2 + h], near_recv.at[7 * p + 2 + h], at_offset(sign[p], 0),
        )

    hop3_parts = [pl.ds(0, side // 2), pl.ds(side // 2, side)]

    def hop3(p, h):
        return send(
            picked.at[p, hop3_parts[h]], land3.at[p, hop3_parts[h]],
            near_send.at[7 * p + 4 + h], near_recv.at[7 * p + 4 + h], at_offset(sign[p], 0),
        )

    def hop4(p):
        return send(
            land3.at[p, hop3_parts[0]], land4.at[p],
            near_send.at[7 * p + 6], near_recv.at[7 * p + 6], at_offset(sign[p], 0),
        )

    sources = [pts_ref, raw1_up, raw1_down, raw2_up, raw2_down]

    def held_at(o, i):
        if o < 5:
            return stage.at[o, i]
        if o < 7:
            return land3.at[o - 5, side // 2 + i]
        return land4.at[i // (side // 2), i % (side // 2)]

    def across_v(o, i):
        return send(
            held_at(o, i), recv.at[o * side + i],
            far_send.at[o * side + i], far_recv.at[o * side + i], at_offset(0, ranked(i)),
        )

    def prepare(o):
        def one(i, carry):
            stage[o, i] = pick(sources[o], o, at_offset(0, ranked(i)))
            return carry

        lax.fori_loop(1, side, one, 0)
        recv[o * side] = pick(sources[o], o, me)

    def spread(o, stop=side):
        def one(i, carry):
            across_v(o, i).start()
            return carry

        lax.fori_loop(1, stop, one, 0)
        if o in (5, 6):
            recv[o * side] = land3[o - 5, side // 2]
        elif o == 7:
            recv[o * side] = land4[0, 0]

    pl.semaphore_wait(barrier, 4 + side - 1 + chips)
    both = (0, 1)
    for h in both:
        for p in both:
            hop1(p, h).start()
    for p in both:
        for d in (1, 2):
            tell(p, d).start()
    load_points.wait()
    prepare(0)
    acc[...] = jnp.zeros_like(acc)
    load_centroids.wait()
    for h in both:
        for p in both:
            hop1(p, h).wait_recv()
            hop2(p, h).start()
    for p in both:
        tell(p, 1).wait_recv()
        prepare(1 + p)
    for p in both:
        tell(p, 2).wait_recv()
        hop2(p, 0).wait_recv()
        hop2(p, 1).wait_recv()

    fillers = 2
    for i in range(side - fillers, side):
        across_v(0, i).start()

    for p in both:

        def beyond(i, carry):
            k = at_offset(2 * sign[p], ranked(p * (side // 2) + i))
            picked[p, i] = pick(raw2[p], 3 + p, k)
            return carry

        lax.fori_loop(0, side // 2, beyond, 0)
        hop3(p, 0).start()
    for p in both:

        def following(i, carry):
            k = at_offset(sign[p], ranked(i))
            picked[p, side // 2 + i] = pick(raw2[p], 3 + p, k)
            return carry

        lax.fori_loop(0, side, following, 0)
        hop3(p, 1).start()
    for p in both:
        prepare(3 + p)
    for p in both:
        hop3(p, 0).wait_recv()
        hop4(p).start()
    for p in both:
        hop3(p, 1).wait_recv()
    spread(0, side - fillers)
    spread(1)
    for p in both:
        hop4(p).wait_recv()
    for o in range(2, side):
        spread(o)

    alpha = 3.0 / math.sqrt(feature) * math.log2(math.e)
    points = GROUP * pts_ref.shape[1]

    def ready(j):
        def arrive(b, carry):
            slot = j * GROUP + b
            pltpu.make_async_copy(recv.at[slot], recv.at[slot], far_recv.at[slot]).wait()
            return carry

        lax.fori_loop(jnp.where((j * GROUP) % side == 0, 1, 0), GROUP, arrive, 0)

    def block(j):
        return recv[pl.ds(j * GROUP, GROUP)].reshape(points, feature)

    def tiles(function, initial):
        return lax.fori_loop(0, rows // TILE, function, initial, unroll=True)

    def exponentials(j):
        def scores(r, top):
            at = pl.ds(pl.multiple_of(r * TILE, TILE), TILE)
            part = lax.dot_general(
                cent_ref[at, :], block(j), (((1,), (1,)), ((), ())),
                preferred_element_type=jnp.float32,
            )
            logit[at, :] = part
            return jnp.maximum(top, jnp.max(part, axis=0, keepdims=True))

        top = tiles(scores, jnp.full((1, points), -jnp.inf, jnp.float32)) * alpha

        def powers(r, total):
            at = pl.ds(pl.multiple_of(r * TILE, TILE), TILE)
            value = jnp.exp2(logit[at, :] * alpha - top)
            logit[at, :] = value
            return total + jnp.sum(value, axis=0, keepdims=True)

        return 1.0 / tiles(powers, jnp.zeros((1, points), jnp.float32))

    def add(j, at, inverse):
        weights = (logit[at, :] * inverse).astype(jnp.bfloat16)
        acc[at, :] += jnp.dot(weights, block(j), preferred_element_type=jnp.float32)

    def step(j, carry):
        ready(j)
        inverse = exponentials(j)

        def sums(r, carry):
            add(j, pl.ds(pl.multiple_of(r * TILE, TILE), TILE), inverse)
            return carry

        tiles(sums, 0)
        return carry

    last = slots // GROUP - 1
    lax.fori_loop(0, last, step, 0)
    ready(last)
    inverse = exponentials(last)

    def across(t, other_core):
        at = pl.ds(pl.multiple_of((2 * t + other_core) * share, share), share)
        return pltpu.make_async_remote_copy(
            src_ref=acc.at[at, :],
            dst_ref=pair.at[t],
            send_sem=pair_send.at[t],
            recv_sem=pair_recv.at[t],
            device_id=(me, partner),
            device_id_type=MESH,
        )

    def ring(d):
        return pltpu.make_async_remote_copy(
            src_ref=sbuf.at[d - 1],
            dst_ref=rbuf.at[d - 1],
            send_sem=ring_send.at[d - 1],
            recv_sem=ring_recv.at[d - 1],
            device_id=(me, ((chip + d) % chips) * 2 + core),
            device_id_type=MESH,
        )

    def chunk(t, of_core):
        return pl.ds(pl.multiple_of((2 * t + of_core) * share, share), share)

    order = [2, 1, 3, 0][:chips]
    for d in order:
        t = (chip + d) % chips
        add(last, chunk(t, 1 - core), inverse)
        across(t, 1 - core).start()
    for d in order:
        t = (chip + d) % chips
        add(last, chunk(t, core), inverse)
        across(t, 1 - core).wait_recv()
        if d:
            sbuf[d - 1] = (acc[chunk(t, core), :] + pair[t]).astype(jnp.bfloat16)
            ring(d).start()
    for p in both:
        for h in both:
            tell(p, 1 + h).wait_send()
            hop1(p, h).wait_send()
            hop2(p, h).wait_send()
            hop3(p, h).wait_send()
        hop4(p).wait_send()
    for o in range(side):

        def sent(i, carry):
            across_v(o, i).wait_send()
            return carry

        lax.fori_loop(1, side, sent, 0)
    for d in order:
        across((chip + d) % chips, 1 - core).wait_send()
    mine = pl.ds(pl.multiple_of(lane * share, share), share)
    value = acc[mine, :] + pair[chip] + cent_ref[mine, :].astype(jnp.float32)
    for d in order:
        if d:
            ring(d).wait_recv()
            value = value + rbuf[d - 1].astype(jnp.float32)
    scale = lax.rsqrt(jnp.mean(value * value, axis=-1, keepdims=True) + 1e-06)
    out_ref[...] = (value * scale).astype(jnp.bfloat16)

    for d in order:
        if d:
            ring(d).wait_send()


def local(points, block_ids, block_counts, centroids):
    held, block_rows, feature = points.shape
    slots = lax.axis_size("cluster")
    copies = lax.axis_size("copy")
    rows = centroids.shape[0]
    share = rows // copies
    chips = copies // 2
    smem = pl.BlockSpec(memory_space=pltpu.SMEM)
    anywhere = pl.BlockSpec(memory_space=pl.ANY)
    vmem = pl.BlockSpec(memory_space=pltpu.VMEM)
    side = int(math.sqrt(slots))
    def blocks(*lead):
        return pltpu.VMEM((*lead, block_rows, feature), jnp.bfloat16)

    dma = pltpu.SemaphoreType.DMA
    return pl.pallas_call(
        functools.partial(kernel, (slots, side, copies)),
        out_shape=jax.ShapeDtypeStruct((share, feature), jnp.bfloat16),
        in_specs=[smem, smem, anywhere, anywhere],
        out_specs=vmem,
        scratch_shapes=[
            pltpu.VMEM(points.shape, jnp.bfloat16),
            pltpu.VMEM(centroids.shape, jnp.bfloat16),
            blocks(held),
            blocks(held),
            blocks(held),
            blocks(held),
            blocks(2, side + side // 2),
            blocks(2, side + side // 2),
            blocks(2, side // 2),
            blocks(5, side),
            blocks(slots),
            pltpu.VMEM((5, 8, 128), jnp.int32),
            pltpu.VMEM((rows, GROUP * block_rows), jnp.float32),
            pltpu.VMEM((rows, feature), jnp.float32),
            pltpu.VMEM((chips, share, feature), jnp.float32),
            pltpu.VMEM((chips - 1, share, feature), jnp.bfloat16),
            pltpu.VMEM((chips - 1, share, feature), jnp.bfloat16),
            dma((14,)),
            dma((14,)),
            dma((4,)),
            dma((4,)),
            dma((slots,)),
            dma((slots,)),
            dma((chips,)),
            dma((chips,)),
            dma((chips - 1,)),
            dma((chips - 1,)),
            dma((2,)),
        ],
        compiler_params=pltpu.CompilerParams(
            collective_id=0, has_side_effects=True, vmem_limit_bytes=56 << 20
        ),
    )(block_ids, block_counts, points, centroids)


def solution(mesh):
    return jax.shard_map(
        local,
        mesh=mesh,
        in_specs=(
            P(("cluster", "copy"), None, None),
            P(("cluster", "copy")),
            P(("cluster", "copy")),
            P("cluster", None),
        ),
        out_specs=P(("cluster", "copy"), None),
        check_vma=False,
    )
```

```python
import functools
import math

import jax
import jax.numpy as jnp
from jax import lax
from jax.experimental import pallas as pl
from jax.experimental.pallas import tpu as pltpu
from jax.sharding import PartitionSpec as P

MESH = pl.DeviceIdType.MESH
GROUP = 4
TILE = 512


def kernel(
    shape, ids_ref, count_ref, points_ref, centroids_ref, out_ref,
    pts_ref, cent_ref, raw1_up, raw1_down, raw2_up, raw2_down, picked, land3, land4,
    stage, recv, names, logit, acc, pair, sbuf, rbuf,
    near_send, near_recv, name_send, name_recv, far_send, far_recv,
    pair_send, pair_recv, ring_send, ring_recv, load_sem,
):
    slots, side, copies = shape
    rows, feature = cent_ref.shape
    held = pts_ref.shape[0]
    half = held // 2
    share = rows // copies
    chips = copies // 2
    me = lax.axis_index("cluster")
    lane = lax.axis_index("copy")
    chip, core = lane // 2, lane % 2
    partner = chip * 2 + (1 - core)
    u = (1 - core) * (me // side) + core * (me % side)
    v = (1 - core) * (me % side) + core * (me // side)

    def at_offset(du, dv):
        a, b = (u + du + side) % side, (v + dv + side) % side
        return (1 - core) * (a * side + b) + core * (b * side + a)

    def ranked(i):
        return jnp.where(i % 2 == 1, (i + 1) // 2, (side - i // 2) % side)

    load_points = pltpu.make_async_copy(points_ref, pts_ref, load_sem.at[0])
    load_centroids = pltpu.make_async_copy(centroids_ref, cent_ref, load_sem.at[1])
    load_points.start()
    load_centroids.start()

    barrier = pltpu.get_barrier_semaphore()

    def signal(cluster, copy):
        pl.semaphore_signal(barrier, inc=1, device_id=(cluster, copy), device_id_type=MESH)

    for d in (1, -1, 2, -2):
        signal(at_offset(d, 0), lane)

    def greet(d, carry):
        signal(at_offset(0, d), lane)
        return carry

    lax.fori_loop(1, side, greet, 0)
    signal(me, partner)
    for d in range(1, chips):
        signal(me, ((chip + d) % chips) * 2 + core)

    count = count_ref[0]
    column = lax.broadcasted_iota(jnp.int32, names.shape[1:], 1)
    listed = jnp.full(names.shape[1:], -1, jnp.int32)
    for n in range(held):
        listed = jnp.where(column == n, jnp.where(count > n, ids_ref[n], -1), listed)
    names[0] = listed

    def pick(source, entry, k):
        code = jnp.max(jnp.where(names[entry] == k, column + 1, 0))
        found = jnp.minimum(code, 1).astype(jnp.float32).astype(jnp.bfloat16)
        return source[jnp.maximum(code - 1, 0)] * found

    def send(src, dst, send_sem, recv_sem, cluster):
        return pltpu.make_async_remote_copy(
            src_ref=src,
            dst_ref=dst,
            send_sem=send_sem,
            recv_sem=recv_sem,
            device_id=(cluster, lane),
            device_id_type=MESH,
        )

    raw1, raw2 = (raw1_up, raw1_down), (raw2_up, raw2_down)
    sign = (1, -1)
    part = [pl.ds(0, half), pl.ds(half, half)]

    def tell(p, d):
        at = 2 * (d - 1) + p
        return send(
            names.at[0], names.at[1 + at], name_send.at[at], name_recv.at[at],
            at_offset(sign[p] * d, 0),
        )

    def hop1(p, h):
        return send(
            points_ref.at[part[h]], raw1[p].at[part[h]],
            near_send.at[7 * p + h], near_recv.at[7 * p + h], at_offset(sign[p], 0),
        )

    def hop2(p, h):
        return send(
            raw1[p].at[part[h]], raw2[p].at[part[h]],
            near_send.at[7 * p + 2 + h], near_recv.at[7 * p + 2 + h], at_offset(sign[p], 0),
        )

    hop3_parts = [pl.ds(0, side // 2), pl.ds(side // 2, side)]

    def hop3(p, h):
        return send(
            picked.at[p, hop3_parts[h]], land3.at[p, hop3_parts[h]],
            near_send.at[7 * p + 4 + h], near_recv.at[7 * p + 4 + h], at_offset(sign[p], 0),
        )

    def hop4(p):
        return send(
            land3.at[p, hop3_parts[0]], land4.at[p],
            near_send.at[7 * p + 6], near_recv.at[7 * p + 6], at_offset(sign[p], 0),
        )

    sources = [pts_ref, raw1_up, raw1_down, raw2_up, raw2_down]

    def held_at(o, i):
        if o < 5:
            return stage.at[o, i]
        if o < 7:
            return land3.at[o - 5, side // 2 + i]
        return land4.at[i // (side // 2), i % (side // 2)]

    def across_v(o, i):
        return send(
            held_at(o, i), recv.at[o * side + i],
            far_send.at[o * side + i], far_recv.at[o * side + i], at_offset(0, ranked(i)),
        )

    def prepare(o):
        def one(i, carry):
            stage[o, i] = pick(sources[o], o, at_offset(0, ranked(i)))
            return carry

        lax.fori_loop(1, side, one, 0)
        recv[o * side] = pick(sources[o], o, me)

    def spread(o, start=1):
        def one(i, carry):
            across_v(o, i).start()
            return carry

        lax.fori_loop(start, side, one, 0)
        if o in (5, 6):
            recv[o * side] = land3[o - 5, side // 2]
        elif o == 7:
            recv[o * side] = land4[0, 0]

    pl.semaphore_wait(barrier, 4 + side - 1 + chips)
    both = (0, 1)
    for h in both:
        for p in both:
            hop1(p, h).start()
    for p in both:
        for d in (1, 2):
            tell(p, d).start()
    load_points.wait()
    prepare(0)
    acc[...] = jnp.zeros_like(acc)
    load_centroids.wait()
    for h in both:
        for p in both:
            hop1(p, h).wait_recv()
            hop2(p, h).start()
    for p in both:
        tell(p, 1).wait_recv()
        prepare(1 + p)
    for p in both:
        tell(p, 2).wait_recv()
        hop2(p, 0).wait_recv()
        hop2(p, 1).wait_recv()

    fillers = 4
    for i in range(1, 1 + fillers):
        across_v(0, i).start()

    for p in both:

        def beyond(i, carry):
            k = at_offset(2 * sign[p], ranked(p * (side // 2) + i))
            picked[p, i] = pick(raw2[p], 3 + p, k)
            return carry

        lax.fori_loop(0, side // 2, beyond, 0)
        hop3(p, 0).start()
    for p in both:

        def following(i, carry):
            k = at_offset(sign[p], ranked(i))
            picked[p, side // 2 + i] = pick(raw2[p], 3 + p, k)
            return carry

        lax.fori_loop(0, side, following, 0)
        hop3(p, 1).start()
    for p in both:
        prepare(3 + p)
    for p in both:
        hop3(p, 0).wait_recv()
        hop4(p).start()
    for p in both:
        hop3(p, 1).wait_recv()
    spread(0, 1 + fillers)
    spread(1)
    for p in both:
        hop4(p).wait_recv()
    for o in range(2, side):
        spread(o)

    alpha = 3.0 / math.sqrt(feature) * math.log2(math.e)
    points = GROUP * pts_ref.shape[1]

    def ready(j):
        def arrive(b, carry):
            slot = j * GROUP + b
            pltpu.make_async_copy(recv.at[slot], recv.at[slot], far_recv.at[slot]).wait()
            return carry

        lax.fori_loop(jnp.where((j * GROUP) % side == 0, 1, 0), GROUP, arrive, 0)

    def block(j):
        return recv[pl.ds(j * GROUP, GROUP)].reshape(points, feature)

    def tiles(function, initial):
        return lax.fori_loop(0, rows // TILE, function, initial, unroll=True)

    def exponentials(j):
        def scores(r, top):
            at = pl.ds(pl.multiple_of(r * TILE, TILE), TILE)
            part = lax.dot_general(
                cent_ref[at, :], block(j), (((1,), (1,)), ((), ())),
                preferred_element_type=jnp.float32,
            )
            logit[at, :] = part
            return jnp.maximum(top, jnp.max(part, axis=0, keepdims=True))

        top = tiles(scores, jnp.full((1, points), -jnp.inf, jnp.float32)) * alpha

        def powers(r, total):
            at = pl.ds(pl.multiple_of(r * TILE, TILE), TILE)
            value = jnp.exp2(logit[at, :] * alpha - top)
            logit[at, :] = value
            return total + jnp.sum(value, axis=0, keepdims=True)

        return 1.0 / tiles(powers, jnp.zeros((1, points), jnp.float32))

    def add(j, at, inverse):
        weights = (logit[at, :] * inverse).astype(jnp.bfloat16)
        acc[at, :] += jnp.dot(weights, block(j), preferred_element_type=jnp.float32)

    def step(j, carry):
        ready(j)
        inverse = exponentials(j)

        def sums(r, carry):
            add(j, pl.ds(pl.multiple_of(r * TILE, TILE), TILE), inverse)
            return carry

        tiles(sums, 0)
        return carry

    last = slots // GROUP - 1
    lax.fori_loop(0, last, step, 0)
    ready(last)
    inverse = exponentials(last)

    def across(t, other_core):
        at = pl.ds(pl.multiple_of((2 * t + other_core) * share, share), share)
        return pltpu.make_async_remote_copy(
            src_ref=acc.at[at, :],
            dst_ref=pair.at[t],
            send_sem=pair_send.at[t],
            recv_sem=pair_recv.at[t],
            device_id=(me, partner),
            device_id_type=MESH,
        )

    def ring(d):
        return pltpu.make_async_remote_copy(
            src_ref=sbuf.at[d - 1],
            dst_ref=rbuf.at[d - 1],
            send_sem=ring_send.at[d - 1],
            recv_sem=ring_recv.at[d - 1],
            device_id=(me, ((chip + d) % chips) * 2 + core),
            device_id_type=MESH,
        )

    def chunk(t, of_core):
        return pl.ds(pl.multiple_of((2 * t + of_core) * share, share), share)

    order = [2, 1, 3, 0][:chips]
    for d in order:
        t = (chip + d) % chips
        add(last, chunk(t, 1 - core), inverse)
        across(t, 1 - core).start()
    for d in order:
        t = (chip + d) % chips
        add(last, chunk(t, core), inverse)
        across(t, 1 - core).wait_recv()
        if d:
            sbuf[d - 1] = (acc[chunk(t, core), :] + pair[t]).astype(jnp.bfloat16)
            ring(d).start()
    for p in both:
        for h in both:
            tell(p, 1 + h).wait_send()
            hop1(p, h).wait_send()
            hop2(p, h).wait_send()
            hop3(p, h).wait_send()
        hop4(p).wait_send()
    for o in range(side):

        def sent(i, carry):
            across_v(o, i).wait_send()
            return carry

        lax.fori_loop(1, side, sent, 0)
    for d in order:
        across((chip + d) % chips, 1 - core).wait_send()
    mine = pl.ds(pl.multiple_of(lane * share, share), share)
    value = acc[mine, :] + pair[chip] + cent_ref[mine, :].astype(jnp.float32)
    for d in order:
        if d:
            ring(d).wait_recv()
            value = value + rbuf[d - 1].astype(jnp.float32)
    scale = lax.rsqrt(jnp.mean(value * value, axis=-1, keepdims=True) + 1e-06)
    out_ref[...] = (value * scale).astype(jnp.bfloat16)

    for d in order:
        if d:
            ring(d).wait_send()


def local(points, block_ids, block_counts, centroids):
    held, block_rows, feature = points.shape
    slots = lax.axis_size("cluster")
    copies = lax.axis_size("copy")
    rows = centroids.shape[0]
    share = rows // copies
    chips = copies // 2
    smem = pl.BlockSpec(memory_space=pltpu.SMEM)
    anywhere = pl.BlockSpec(memory_space=pl.ANY)
    vmem = pl.BlockSpec(memory_space=pltpu.VMEM)
    side = int(math.sqrt(slots))
    def blocks(*lead):
        return pltpu.VMEM((*lead, block_rows, feature), jnp.bfloat16)

    dma = pltpu.SemaphoreType.DMA
    return pl.pallas_call(
        functools.partial(kernel, (slots, side, copies)),
        out_shape=jax.ShapeDtypeStruct((share, feature), jnp.bfloat16),
        in_specs=[smem, smem, anywhere, anywhere],
        out_specs=vmem,
        scratch_shapes=[
            pltpu.VMEM(points.shape, jnp.bfloat16),
            pltpu.VMEM(centroids.shape, jnp.bfloat16),
            blocks(held),
            blocks(held),
            blocks(held),
            blocks(held),
            blocks(2, side + side // 2),
            blocks(2, side + side // 2),
            blocks(2, side // 2),
            blocks(5, side),
            blocks(slots),
            pltpu.VMEM((5, 8, 128), jnp.int32),
            pltpu.VMEM((rows, GROUP * block_rows), jnp.float32),
            pltpu.VMEM((rows, feature), jnp.float32),
            pltpu.VMEM((chips, share, feature), jnp.float32),
            pltpu.VMEM((chips - 1, share, feature), jnp.bfloat16),
            pltpu.VMEM((chips - 1, share, feature), jnp.bfloat16),
            dma((14,)),
            dma((14,)),
            dma((4,)),
            dma((4,)),
            dma((slots,)),
            dma((slots,)),
            dma((chips,)),
            dma((chips,)),
            dma((chips - 1,)),
            dma((chips - 1,)),
            dma((2,)),
        ],
        compiler_params=pltpu.CompilerParams(
            collective_id=0, has_side_effects=True, vmem_limit_bytes=56 << 20
        ),
    )(block_ids, block_counts, points, centroids)


def solution(mesh):
    return jax.shard_map(
        local,
        mesh=mesh,
        in_specs=(
            P(("cluster", "copy"), None, None),
            P(("cluster", "copy")),
            P(("cluster", "copy")),
            P("cluster", None),
        ),
        out_specs=P(("cluster", "copy"), None),
        check_vma=False,
    )
```
